32 devices in a mesh: expert: 8 (over z, y), batch: 4 (over x, core).
Axes of the slice: x: 2, y: 2, z: 4, core: 2. Of those that a mesh axis runs over, the one named last changes fastest.
Arguments:
- tokens: bfloat16 [8192, 1024], P(('expert', 'batch')), may hold values from -6 to 6
- routes: int32 [8192, 1], P(('expert', 'batch')), may hold values from 0 to 7; in each aligned block of 256 rows (0 to 255, 256 to 511, ...) at most 64 rows name the same one
- centroid: bfloat16 [8, 1024], P('expert'), may hold values from -0.1875 to 0.1875
- ln_gain: bfloat16 [8, 1024], P('expert'), may hold values from 0.099609375 to 1.8984375
- ln_bias: bfloat16 [8, 1024], P('expert'), may hold values from -3 to 3
- w_in: bfloat16 [8, 1024, 4096], P('expert', None, 'batch'), may hold values from -0.1875 to 0.1875
- b_in: bfloat16 [8, 4096], P('expert', 'batch'), may hold values from -3 to 3
- w_out: bfloat16 [8, 4096, 1024], P('expert', 'batch'), may hold values from -0.09375 to 0.09375
- b_out: bfloat16 [8, 1024], P('expert'), may hold values from -3 to 3
- cotangent: bfloat16 [8192, 1024], P(('expert', 'batch')), may hold values from -6 to 6
Outputs:
- mixed: bfloat16 [8192, 1024], P(('expert', 'batch'))
- tokens_grad: float32 [8192, 1024], P(('expert', 'batch'))
- centroid_grad: float32 [8, 1024], P('expert')
- gain_grad: float32 [8, 1024], P('expert')
- bias_grad: float32 [8, 1024], P('expert')
- w_in_grad: float32 [8, 1024, 4096], P('expert', None, 'batch')
- b_in_grad: float32 [8, 4096], P('expert', 'batch')
- w_out_grad: float32 [8, 4096, 1024], P('expert', 'batch')
- b_out_grad: float32 [8, 1024], P('expert')
The draws below stay inside these ranges and needn't reach their ends.
Inputs may be any that keep to these rules, and one draw needn't show every extreme that they name: `routes`: in each aligned block of 256 rows (one device's tokens) no expert is named more than 64 times, a bound that some block reaches.
All inputs are finite; a program needn't handle non-finite values.
Results may differ from the reference program's by a relative error of at most 0.0062.
Values may be sent and summed in bfloat16 or wider, within the bound.
No kernel may reach another device: no remote copies, remote signals or barrier semaphores. Data moves between devices by JAX's collectives and lax.ppermute only.
A program may use at most 128 MiB of HBM per device.

```python
import math
import jax
import jax.numpy as jnp
import numpy as np
from jax import lax

D = 1024
FF = 4096
TOK_DEV = 256
EXPERTS = 8
CAP = 64
TOKENS = 8192


def block_levels(own_key, dims, split, smallest, high):
    loudness = 1.0
    for dim, shards_of in split:
        heights = jax.random.uniform(jax.random.fold_in(jax.random.fold_in(own_key, 6), dim), (shards_of,), jnp.float32, smallest / len(split), high / len(split))
        loudness = loudness * jnp.repeat(jnp.exp(heights), dims[dim] // shards_of).reshape((-1,) + (1,) * (len(dims) - 1 - dim))
    return loudness


def routed_block(rng, own, number, rows, amount, top, limit, lean):
    ranking = jax.random.permutation(rng, amount)
    crowded, common = shares(amount, rows * top, limit, lean, True), shares(amount, rows * top, limit, lean, False)
    places = jnp.arange(amount)

    def named(tallies, offset_by):
        used = int((tallies > 0).sum())
        fixed = max(1, used // 4)
        moved = fixed + (places - fixed + offset_by * (used - fixed)) % max(1, amount - fixed)
        return jnp.zeros((amount,), jnp.int32).at[ranking[jnp.where(places < fixed, places, moved)]].set(jnp.asarray(tallies, jnp.int32))

    tallies = jnp.where(number % 4 == 0, named(crowded, number // 4), named(common, number - number // 4 - 1))
    mixed = jax.random.permutation(jax.random.fold_in(own, 3), amount)
    giver, sink = mixed[0:amount // 2 * 2:2], mixed[1:amount // 2 * 2:2]
    room = jnp.minimum(tallies[giver] - 1, limit - tallies[sink]) // 2
    room = jnp.where((giver == ranking[0]) | (sink == ranking[0]) | (tallies[sink] == 0), 0, jnp.maximum(room, 0))
    moved = jax.random.randint(jax.random.fold_in(own, 4), (amount // 2,), 0, 1 << 20) % (room + 1)
    tallies = tallies.at[giver].add(-moved).at[sink].add(moved)
    members = jnp.searchsorted(jnp.cumsum(tallies), jnp.arange(rows * top), side="right").astype(jnp.int32)
    listing = members.reshape(top, rows).T
    listing = listing[jax.random.permutation(jax.random.fold_in(own, 1), rows)]
    offset_by = jax.random.randint(jax.random.fold_in(own, 2), (rows, 1), 0, top)
    return jnp.take_along_axis(listing, (jnp.arange(top)[None, :] + offset_by) % top, axis=1)


def shares(count, total, limit, slope, full):
    weights = [(1 << 20) // math.isqrt(rank ** slope) + 1 for rank in range(1, count + 1)]
    largest = limit if full else min(limit, max(-(-total // count), total * weights[0] // sum(weights)))
    least = 1 if total - largest >= count - 1 else 0
    holding, spare = [largest] + [least] * (count - 1), total - largest - least * (count - 1)
    while spare > 0:
        candidates = [i for i in range(1, count) if holding[i] < largest] or [i for i in range(1, count) if holding[i] < limit]
        pool, left = sum([weights[i] for i in candidates]), spare
        for i in candidates:
            addition = min(limit - holding[i], max(1, left * weights[i] // pool), spare)
            holding[i] = holding[i] + addition
            spare = spare - addition
    return np.array(holding)


def bell_draw(key, shape, scale, most, cuts=(), kind=jnp.bfloat16):
    drawn = jax.random.normal(key, shape, jnp.float32) * scale
    if len(cuts) > 0:
        drawn = block_levels(key, shape, cuts, -0.22, 0.18) * drawn
    return jnp.clip(drawn, min=-most, max=most).astype(kind)


def setup_inputs(seed: int = 0) -> dict:
    splits = jax.random.split(jax.random.key(seed), 11)
    tokens = bell_draw(splits[0], (TOKENS, D), 1.0, 6.0, ((0, 32),))
    routes_keys = jax.random.split(jax.random.fold_in(splits[1], 1), TOKENS // TOK_DEV)
    routes_turns = jax.random.permutation(jax.random.fold_in(splits[1], 3), TOKENS // TOK_DEV)
    routes = jax.vmap(lambda own, number: routed_block(jax.random.fold_in(splits[1], 2), own, number, TOK_DEV, EXPERTS, 1, CAP, 2))(routes_keys, routes_turns).reshape((TOKENS, 1))
    centroid = bell_draw(splits[2], (EXPERTS, D), D ** -0.5, 0.1875, ((0, 8),))
    ln_gain = jnp.clip(1.0 + 0.18 * jax.random.normal(splits[3], (EXPERTS, D), jnp.float32), 0.099609375, 1.8984375).astype(jnp.bfloat16)
    ln_bias = bell_draw(splits[4], (EXPERTS, D), 0.5, 3.0, ((0, 8),))
    w_in = bell_draw(splits[5], (EXPERTS, D, FF), D ** -0.5, 0.1875, ((0, 8), (2, 4)))
    b_in = bell_draw(splits[6], (EXPERTS, FF), 0.5, 3.0, ((0, 8), (1, 4)))
    w_out = bell_draw(splits[7], (EXPERTS, FF, D), FF ** -0.5, 0.09375, ((0, 8), (1, 4)))
    b_out = bell_draw(splits[8], (EXPERTS, D), 0.5, 3.0, ((0, 8),))
    cotangent = bell_draw(splits[9], (TOKENS, D), 1.0, 6.0, ((0, 32),))
    return dict(tokens=tokens, routes=routes, centroid=centroid, ln_gain=ln_gain, ln_bias=ln_bias, w_in=w_in, b_in=b_in, w_out=w_out, b_out=b_out, cotangent=cotangent)


@jax.custom_vjp
def low(v):
    return lax.optimization_barrier(v.astype(jnp.bfloat16)).astype(jnp.float32)

@jax.custom_vjp
def low_back(v):
    return v

def low_keep(v):
    return (low(v), None)

def low_pass(kept, grad):
    return (grad,)

def back_keep(v):
    return (v, None)

def back_low(kept, grad):
    return (low(grad),)
low.defvjp(low_keep, low_pass)
low_back.defvjp(back_keep, back_low)
epsilon = 1e-05

def expert_rows(pieces):
    rows_in, cent_row, gain_row, shift_row, first_w, first_b, second_w, second_b = pieces
    center = lax.optimization_barrier(jnp.mean(rows_in, axis=1, keepdims=True))
    spread = lax.optimization_barrier(jnp.mean((rows_in - center) * (rows_in - center), axis=1, keepdims=True))
    normed = (rows_in - center) * lax.rsqrt(spread + epsilon)
    lowered = low(normed * gain_row + shift_row)
    pre_act = low_back(jnp.dot(lowered, first_w, precision=lax.Precision.HIGHEST) + first_b)
    activated = low(jax.nn.gelu(pre_act, approximate=False))
    branch = low_back(jnp.dot(activated, second_w, precision=lax.Precision.HIGHEST) + second_b)
    mixing = jax.nn.sigmoid(jnp.dot(rows_in, cent_row, precision=lax.Precision.HIGHEST))
    return low(low_back(mixing[:, None] * (rows_in + branch)))

def reference(tokens, routes, centroid, ln_gain, ln_bias, w_in, b_in, w_out, b_out, cotangent):
    route_ids = routes[:, 0].astype(jnp.int32)
    blocks = route_ids.reshape(-1, TOK_DEV)
    onehot = (blocks[:, :, None] == jnp.arange(EXPERTS, dtype=jnp.int32)[None, None, :]).astype(jnp.int32)
    rank_in = lax.optimization_barrier(jnp.sum((jnp.cumsum(onehot, axis=1) - onehot) * onehot, axis=2))
    block_ids = jnp.arange(blocks.shape[0], dtype=jnp.int32)[:, None]
    slot_of = (block_ids * CAP + rank_in).reshape(-1).astype(jnp.int32)
    per_expert = blocks.shape[0] * CAP
    position = (route_ids * per_expert + slot_of).astype(jnp.int32)
    total = tokens.shape[0]
    source_row = jnp.zeros((EXPERTS * per_expert,), jnp.int32).at[position].set(jnp.arange(total, dtype=jnp.int32))
    filled = jnp.zeros((EXPERTS * per_expert,), jnp.float32).at[position].set(1.0)

    def forward(inputs, cent, gains, shifts, first_w, first_b, second_w, second_b):
        routed = low_back(inputs)
        buffer = (routed[source_row] * filled[:, None]).reshape(EXPERTS, per_expert, D)
        results = lax.map(jax.checkpoint(expert_rows), (buffer, cent, gains, shifts, first_w, first_b, second_w, second_b))
        return inputs + results.reshape(-1, D)[position]
    floats = [tokens.astype(jnp.float32), centroid.astype(jnp.float32), ln_gain.astype(jnp.float32), ln_bias.astype(jnp.float32), w_in.astype(jnp.float32), b_in.astype(jnp.float32), w_out.astype(jnp.float32), b_out.astype(jnp.float32)]
    layer_out, pullback = jax.vjp(forward, *floats)
    gradients = pullback(cotangent.astype(jnp.float32))
    return (layer_out.astype(jnp.bfloat16), gradients[0], gradients[1], gradients[2], gradients[3], gradients[4], gradients[5], gradients[6], gradients[7])
```

```python
import functools

import jax
import jax.numpy as jnp
from jax import lax
from jax.experimental import pallas as pl
from jax.experimental.pallas import tpu as pltpu
from jax.sharding import PartitionSpec as P

epsilon = 1e-05
root_half = 0.7071067811865476
gauss_norm = 0.3989422804014327


def gelu_parts(pre_act):
    gelu_value = jax.nn.gelu(pre_act, approximate=False)
    gelu_slope = (
        0.5 * (1.0 + lax.erf(pre_act * root_half))
        + pre_act * jnp.exp(-0.5 * pre_act * pre_act) * gauss_norm
    )
    return (gelu_value.astype(jnp.bfloat16), gelu_slope)


def contract_first(left, right):
    return lax.dot_general(
        left, right, (((0,), (0,)), ((), ())), preferred_element_type=jnp.float32
    )


def contract_last(left, right):
    return lax.dot_general(
        left, right, (((1,), (1,)), ((), ())), preferred_element_type=jnp.float32
    )


def local_general(tokens, routes, centroid, ln_gain, ln_bias, w_in, b_in, w_out, b_out, cotangent):
    experts = lax.axis_size("expert")
    tok_count = tokens.shape[0]
    model_width = tokens.shape[1]
    capacity = max(2, 2 * tok_count // experts)
    row_count = experts * capacity
    route_ids = routes[:, 0]
    onehot = (route_ids[:, None] == jnp.arange(experts, dtype=jnp.int32)[None, :]).astype(jnp.int32)
    before = jnp.cumsum(onehot, axis=0) - onehot
    rank_in = jnp.sum(before * onehot, axis=1)
    target = route_ids * capacity + rank_in
    placing = (jnp.arange(row_count, dtype=jnp.int32)[:, None] == target[None, :]).astype(
        jnp.bfloat16
    )
    outgoing = jnp.dot(placing, tokens, preferred_element_type=jnp.float32).astype(jnp.bfloat16)
    arrived = lax.all_to_all(
        outgoing.reshape(experts, capacity, model_width),
        "expert",
        split_axis=0,
        concat_axis=0,
        tiled=True,
    )
    arrived = arrived.reshape(row_count, model_width)
    hidden_in = arrived.astype(jnp.float32)
    center = jnp.mean(hidden_in, axis=1, keepdims=True)
    spread = jnp.mean((hidden_in - center) * (hidden_in - center), axis=1, keepdims=True)
    inv_std = lax.rsqrt(spread + epsilon)
    normed = (hidden_in - center) * inv_std
    gain_row = ln_gain[0].astype(jnp.float32)
    shift_row = ln_bias[0].astype(jnp.float32)
    cent_row = centroid[0].astype(jnp.float32)
    b_last = b_out[0].astype(jnp.float32)
    lowered = (normed * gain_row + shift_row).astype(jnp.bfloat16)
    gate_logit = jnp.dot(arrived, centroid[0], preferred_element_type=jnp.float32)
    mixing = jax.nn.sigmoid(gate_logit)
    w_first = w_in[0]
    w_second = w_out[0]
    b_first = b_in[0].astype(jnp.float32)
    inputs_all = lax.all_gather(lowered, "batch", axis=0, tiled=True)
    row_piece = inputs_all
    piece_act, unused = gelu_parts(
        jnp.dot(row_piece, w_first, preferred_element_type=jnp.float32) + b_first
    )
    branch = (
        lax.psum_scatter(
            jnp.dot(piece_act, w_second, preferred_element_type=jnp.float32).astype(jnp.bfloat16),
            "batch",
            scatter_dimension=0,
            tiled=True,
        ).astype(jnp.float32)
        + b_last
    )
    expert_out = hidden_in + branch
    reply_rows = (mixing[:, None] * expert_out).astype(jnp.bfloat16)
    returned = lax.all_to_all(
        reply_rows.reshape(experts, capacity, model_width),
        "expert",
        split_axis=0,
        concat_axis=0,
        tiled=True,
    )
    returned = returned.reshape(row_count, model_width)
    mixed = (tokens.astype(jnp.float32) + contract_first(placing, returned)).astype(jnp.bfloat16)
    grad_out = jnp.dot(placing, cotangent, preferred_element_type=jnp.float32).astype(jnp.bfloat16)
    grad_rows = lax.all_to_all(
        grad_out.reshape(experts, capacity, model_width),
        "expert",
        split_axis=0,
        concat_axis=0,
        tiled=True,
    )
    grad_rows = grad_rows.reshape(row_count, model_width).astype(jnp.float32)
    gate_grad = jnp.sum(grad_rows * expert_out, axis=1) * mixing * (1.0 - mixing)
    direct = grad_rows * mixing[:, None]
    branch_grad = direct.astype(jnp.bfloat16)
    b_out_part = jnp.sum(branch_grad.astype(jnp.float32), axis=0)
    centroid_part = jnp.sum(gate_grad[:, None] * hidden_in, axis=0)
    grads_all = lax.all_gather(branch_grad, "batch", axis=0, tiled=True)
    activated, gelu_slope = gelu_parts(
        jnp.dot(inputs_all, w_first, preferred_element_type=jnp.float32) + b_first
    )
    pre_grad = (contract_last(grads_all, w_second) * gelu_slope).astype(jnp.bfloat16)
    w_out_grad = contract_first(activated, grads_all)
    w_in_grad = contract_first(inputs_all, pre_grad)
    b_in_grad = jnp.sum(pre_grad.astype(jnp.float32), axis=0)
    row_piece = pre_grad
    normed_grad = lax.psum_scatter(
        contract_last(row_piece, w_first), "batch", scatter_dimension=0, tiled=True
    )
    gain_part = jnp.sum(normed_grad * normed, axis=0)
    bias_part = jnp.sum(normed_grad, axis=0)
    scaled = normed_grad * gain_row
    ln_grad = inv_std * (
        scaled
        - jnp.mean(scaled, axis=1, keepdims=True)
        - normed * jnp.mean(scaled * normed, axis=1, keepdims=True)
    )
    input_grad = direct + gate_grad[:, None] * cent_row + ln_grad
    outgoing_grads = input_grad.astype(jnp.bfloat16).reshape(experts, capacity, model_width)
    arrived_grads = lax.all_to_all(
        outgoing_grads, "expert", split_axis=0, concat_axis=0, tiled=True
    ).reshape(row_count, model_width)
    tokens_grad = cotangent.astype(jnp.float32) + contract_first(placing, arrived_grads)
    small_sums = lax.psum((centroid_part, gain_part, bias_part, b_out_part), "batch")
    return (
        mixed,
        tokens_grad,
        small_sums[0][None],
        small_sums[1][None],
        small_sums[2][None],
        w_in_grad[None],
        b_in_grad[None],
        w_out_grad[None],
        small_sums[3][None],
    )


f32 = jnp.float32
bf16 = jnp.bfloat16

erfc_step = 0.3 * root_half
erfc_half = tuple(
    0.5 * c
    for c in (
        0.16918935705144628,
        0.1706908732382945,
        0.14852168107322075,
        0.21417961390291307,
        -0.09282143256694776,
        0.5449597059025907,
        -0.5097655323576785,
        0.48429815524087755,
        -0.12925243016104992,
    )
)


def gelu_and_slope(a):
    bell = jnp.exp(-0.5 * a * a)
    t = 1.0 / (1.0 + erfc_step * jnp.abs(a))
    poly = erfc_half[-1]
    for c in erfc_half[-2::-1]:
        poly = poly * t + c
    tail = poly * t * bell
    below = jnp.where(a < 0.0, tail, 1.0 - tail)
    return a * below, below + a * bell * gauss_norm


def whole():
    return pl.BlockSpec(memory_space=pltpu.VMEM)


def call(body, outs, args, name, scratch=(), scalars=0, flops=0, limit=12 << 20):
    moved = sum(x.size * x.dtype.itemsize for x in args) + sum(
        x.size * x.dtype.itemsize for x in outs
    )
    return pl.pallas_call(
        body,
        out_shape=tuple(outs),
        in_specs=[pl.BlockSpec(memory_space=pltpu.SMEM)] * scalars
        + [whole()] * (len(args) - scalars),
        out_specs=tuple(whole() for _ in outs),
        scratch_shapes=list(scratch),
        compiler_params=pltpu.CompilerParams(vmem_limit_bytes=limit),
        cost_estimate=pl.CostEstimate(flops=flops, bytes_accessed=moved, transcendentals=0),
        name=name,
    )(*args)


def out(rows, cols, dtype):
    return jax.ShapeDtypeStruct((rows, cols), dtype)


def iota(shape, dim):
    return lax.broadcasted_iota(jnp.int32, shape, dim)


def slot_row(capacity, me, row):
    n = row.shape[1]
    wide = jnp.broadcast_to(row, (n, n))
    i, j = iota((n, n), 0), iota((n, n), 1)
    col = jnp.sum(jnp.where(i == j, wide, 0), axis=1, keepdims=True)
    rank = jnp.sum(((col == wide) & (i < j)).astype(jnp.int32), axis=0, keepdims=True)
    return jnp.bitwise_xor(row, me) * capacity + rank


def slot_col(capacity, me, row):
    n = row.shape[1]
    wide = jnp.broadcast_to(row, (n, n))
    i, j = iota((n, n), 0), iota((n, n), 1)
    col = jnp.sum(jnp.where(i == j, wide, 0), axis=1, keepdims=True)
    rank = jnp.sum(((col == wide) & (j < i)).astype(jnp.int32), axis=1, keepdims=True)
    return jnp.bitwise_xor(col, me) * capacity + rank


def dispatch_body(capacity, me, routes, tokens, cotangent, *parts):
    slots = len(parts) * capacity
    n = routes.shape[1]
    slot = slot_row(capacity, me[0], routes[...])
    place = (iota((slots, n), 0) == jnp.broadcast_to(slot, (slots, n))).astype(bf16)
    rows = jnp.dot(place, tokens[...], preferred_element_type=f32).astype(bf16)
    grads = jnp.dot(place, cotangent[...], preferred_element_type=f32).astype(bf16)
    for d, part in enumerate(parts):
        part[0:capacity, :] = rows[d * capacity : (d + 1) * capacity, :]
        part[capacity:, :] = grads[d * capacity : (d + 1) * capacity, :]


def row_mean(x):
    return jnp.mean(x, axis=1, keepdims=True)


def norm_parts(h):
    center = row_mean(h)
    spread = row_mean((h - center) * (h - center))
    inv_std = lax.rsqrt(spread + epsilon)
    return (h - center) * inv_std, inv_std


def gate(h, cent):
    return jax.nn.sigmoid(jnp.sum(h * cent, axis=1, keepdims=True))


def enter_body(capacity, count, *refs):
    parts, (cent, gain, shift, both) = refs[:count], refs[count:]
    half = count * capacity
    for j, part in enumerate(parts):
        h = part[0:capacity, :].astype(f32)
        normed, unused = norm_parts(h)
        lowered = normed * gain[...].astype(f32) + shift[...].astype(f32)
        at = j * capacity
        both[at : at + capacity, :] = lowered.astype(bf16)
        mixing = gate(h, cent[...].astype(f32))
        both[half + at : half + at + capacity, :] = (
            part[capacity:, :].astype(f32) * mixing
        ).astype(bf16)


def middle_body(half, first, *refs):
    (own, other, wi0, wo0, wi1, wo1, b0, b1), refs = refs[:8], refs[8:]
    if not first:
        before, refs = refs[0], refs[1:]
    keep, send, n_all, dz_all, u0, da0, u1, da1, sums, z_acc, dn_acc = refs
    n_all[0:half, :] = own[0:half, :]
    n_all[half:, :] = other[0:half, :]
    dz_all[0:half, :] = own[half:, :]
    dz_all[half:, :] = other[half:, :]
    for q, (wi, wo, b, u_ref, da_ref) in enumerate(
        ((wi0, wo0, b0, u0, da0), (wi1, wo1, b1, u1, da1))
    ):
        a = jnp.dot(n_all[...], wi[...], preferred_element_type=f32) + b[...].astype(f32)
        u, slope = gelu_and_slope(a)
        u = u.astype(bf16)
        u_ref[...] = u
        z = jnp.dot(u, wo[...], preferred_element_type=f32)
        da = (contract_last(dz_all[...], wo[...]) * slope).astype(bf16)
        da_ref[...] = da
        dn = contract_last(da, wi[...])
        total = jnp.sum(da.astype(f32), axis=0, keepdims=True)
        if not first:
            total = total + before[q : q + 1, :]
        sums[q : q + 1, :] = total
        if q == 0:
            z_acc[...] = z
            dn_acc[...] = dn
        else:
            z_acc[...] += z
            dn_acc[...] += dn
    sums[2:, :] = jnp.zeros_like(sums[2:, :])
    keep[0:half, :] = z_acc[0:half, :]
    keep[half:, :] = dn_acc[0:half, :]
    send[0:half, :] = z_acc[half:, :].astype(bf16)
    send[half:, :] = dn_acc[half:, :].astype(bf16)


def leave_body(capacity, count, first, last, *refs):
    parts, refs = refs[:count], refs[count:]
    (keep, came, cent, gain, b_out), refs = refs[:5], refs[5:]
    if not first:
        before, refs = refs[0], refs[1:]
    if last:
        hidden_sums, refs = refs[0], refs[1:]
    replies, sums = refs[:count], refs[count]
    half = count * capacity
    cent_row, gain_row = cent[...].astype(f32), gain[...].astype(f32)
    totals = [0.0, 0.0, 0.0, 0.0]
    for j, part in enumerate(parts):
        at = j * capacity
        h = part[0:capacity, :].astype(f32)
        g = part[capacity:, :].astype(f32)
        z = keep[at : at + capacity, :] + came[at : at + capacity, :].astype(f32)
        dn = (
            keep[half + at : half + at + capacity, :]
            + came[half + at : half + at + capacity, :].astype(f32)
        )
        f = h + (z + b_out[...].astype(f32))
        mixing = gate(h, cent_row)
        replies[j][0:capacity, :] = (mixing * f).astype(bf16)
        p = jnp.sum(g * f, axis=1, keepdims=True) * mixing * (1.0 - mixing)
        direct = g * mixing
        normed, inv_std = norm_parts(h)
        w = dn * gain_row
        dh = (
            direct
            + p * cent_row
            + inv_std * (w - row_mean(w) - normed * row_mean(w * normed))
        )
        replies[j][capacity:, :] = dh.astype(bf16)
        for i, rows in enumerate((p * h, dn * normed, dn, direct.astype(bf16).astype(f32))):
            totals[i] = totals[i] + jnp.sum(rows, axis=0, keepdims=True)
    for i, total in enumerate(totals):
        if not first:
            total = total + before[i : i + 1, :]
        sums[i : i + 1, :] = total
    if last:
        sums[4:6, :] = hidden_sums[0:2, :]
        sums[6:, :] = jnp.zeros_like(sums[6:, :])
    else:
        sums[4:, :] = jnp.zeros_like(sums[4:, :])


def weights_body(chunks, *refs):
    u, da, n, dz = (refs[i * chunks : (i + 1) * chunks] for i in range(4))
    rest = refs[4 * chunks :]
    w_in_grad, w_out_grad = rest[-2:]
    for left, right, grad, share in (
        (u, dz, w_out_grad, rest[1]),
        (n, da, w_in_grad, rest[0]),
    ):
        right = jnp.concatenate([x[...] for x in right], axis=0)
        width = left[0].shape[1]
        step = min(512, width)
        for at in range(0, width, step):
            sl = slice(at, at + step)
            total = contract_first(jnp.concatenate([x[:, sl] for x in left], axis=0), right)
            if len(rest) == 4:
                total = total + share[sl, :].astype(f32)
            grad[sl, :] = total.astype(grad.dtype)


def combine_body(capacity, me, routes, tokens, cotangent, *refs):
    replies, (mixed, tokens_grad) = refs[:-2], refs[-2:]
    slots = len(replies) * capacity
    n = routes.shape[1]
    slot = slot_col(capacity, me[0], routes[...])
    place = (iota((n, slots), 1) == jnp.broadcast_to(slot, (n, slots))).astype(bf16)
    rows = jnp.concatenate([x[0:capacity, :] for x in replies], axis=0)
    grads = jnp.concatenate([x[capacity:, :] for x in replies], axis=0)
    mixed[...] = (
        tokens[...].astype(f32) + jnp.dot(place, rows, preferred_element_type=f32)
    ).astype(bf16)
    tokens_grad[...] = cotangent[...].astype(f32) + jnp.dot(
        place, grads, preferred_element_type=f32
    )


def exchange(x, axis, offset):
    size = lax.axis_size(axis)
    return lax.ppermute(x, axis, [(i, i ^ offset) for i in range(size)])


def local_paired(tokens, routes, centroid, ln_gain, ln_bias, w_in, b_in, w_out, b_out, cotangent):
    experts = lax.axis_size("expert")
    tok_count, width = tokens.shape
    capacity = 2 * tok_count // experts
    hidden = w_in.shape[2]
    core, chip = 1, 2
    me = lax.axis_index("expert").astype(jnp.int32).reshape(1)
    route_row = routes.reshape(1, tok_count)
    wi0, wo0 = w_in[0], w_out[0]
    wi1, wo1 = exchange(wi0, "batch", core), exchange(wo0, "batch", core)
    b1 = exchange(b_in, "batch", core)

    outgoing = call(
        functools.partial(dispatch_body, capacity),
        [out(2 * capacity, width, bf16)] * experts,
        (me, route_row, tokens, cotangent),
        "dispatch",
        scalars=1,
        flops=8 * tok_count * tok_count * width,
    )
    arrived = [outgoing[0]] + [
        exchange(outgoing[d], "expert", d) for d in range(1, experts)
    ]
    per_chunk = max(1, 128 // capacity)
    chunks = [list(range(d, d + per_chunk)) for d in range(0, experts, per_chunk)]
    half = per_chunk * capacity
    entered = []
    for ds in chunks:
        both = call(
            functools.partial(enter_body, capacity, per_chunk),
            [out(2 * half, width, bf16)],
            (*[arrived[d] for d in ds], centroid, ln_gain, ln_bias),
            "enter",
        )[0]
        entered.append((both, exchange(both, "batch", chip)))
    done = []
    for c, (both, other) in enumerate(entered):
        wide = [out(2 * half, width, bf16)] * 2 + [out(2 * half, hidden, bf16)] * 4
        done.append(
            call(
                functools.partial(middle_body, half, c == 0),
                [out(2 * half, width, f32), out(2 * half, width, bf16)]
                + wide
                + [out(8, hidden, f32)],
                (both, other, wi0, wo0, wi1, wo1, b_in, b1)
                + (() if c == 0 else (done[-1][8],)),
                "middle",
                scratch=[pltpu.VMEM((2 * half, width), f32)] * 2,
                flops=32 * half * width * hidden,
                limit=24 << 20,
            )
        )
    replies = {}
    sums = None
    for c, ds in enumerate(chunks):
        keep, send = done[c][:2]
        first, last = c == 0, c == len(chunks) - 1
        *sent, sums = call(
            functools.partial(leave_body, capacity, per_chunk, first, last),
            [out(2 * capacity, width, bf16)] * per_chunk + [out(8, width, f32)],
            (
                *[arrived[d] for d in ds],
                keep,
                exchange(send, "batch", chip),
                centroid,
                ln_gain,
                b_out,
                *(() if first else (sums,)),
                *((done[-1][8],) if last else ()),
            ),
            "leave",
        )
        for d, x in zip(ds, sent):
            replies[d] = x if d == 0 else exchange(x, "expert", d)

    n_all, dz_all, u0, da0, u1, da1 = ([x[i] for x in done] for i in range(2, 8))
    flops = 8 * len(chunks) * half * width * hidden
    shares = call(
        functools.partial(weights_body, len(chunks)),
        [out(width, hidden, bf16), out(hidden, width, bf16)],
        (*u1, *da1, *n_all, *dz_all),
        "sibling_weights",
        flops=flops,
    )
    shares = [exchange(x, "batch", core) for x in shares]
    w_in_grad, w_out_grad = call(
        functools.partial(weights_body, len(chunks)),
        [out(width, hidden, f32), out(hidden, width, f32)],
        (*u0, *da0, *n_all, *dz_all, *shares),
        "own_weights",
        flops=flops,
    )
    sums_core = exchange(sums, "batch", core)
    b_in_grad = sums[4:5] + sums_core[5:6]
    sums = sums + sums_core
    sums = sums + exchange(sums, "batch", chip)
    mixed, tokens_grad = call(
        functools.partial(combine_body, capacity),
        [out(tok_count, width, bf16), out(tok_count, width, f32)],
        (me, route_row, tokens, cotangent, *[replies[d] for d in range(experts)]),
        "combine",
        scalars=1,
        flops=8 * tok_count * tok_count * width,
    )
    return (
        mixed,
        tokens_grad,
        sums[0:1],
        sums[1:2],
        sums[2:3],
        w_in_grad[None],
        b_in_grad,
        w_out_grad[None],
        sums[3:4],
    )


def local(tokens, routes, centroid, ln_gain, ln_bias, w_in, b_in, w_out, b_out, cotangent):
    experts = lax.axis_size("expert")
    tok_count, width = tokens.shape
    capacity = 2 * tok_count // experts
    power_of_two = experts & (experts - 1) == 0
    paired = (
        lax.axis_size("batch") == 4
        and power_of_two
        and capacity % 16 == 0
        and capacity <= 128
        and width == w_in.shape[2]
        and width % 128 == 0
    )
    plan = local_paired if paired else local_general
    return plan(
        tokens, routes, centroid, ln_gain, ln_bias, w_in, b_in, w_out, b_out, cotangent
    )


def solution(mesh):
    in_specs = (
        P(("expert", "batch"), None),
        P(("expert", "batch"), None),
        P("expert", None),
        P("expert", None),
        P("expert", None),
        P("expert", None, "batch"),
        P("expert", "batch"),
        P("expert", "batch", None),
        P("expert", None),
        P(("expert", "batch"), None),
    )
    out_specs = (
        P(("expert", "batch"), None),
        P(("expert", "batch"), None),
        P("expert", None),
        P("expert", None),
        P("expert", None),
        P("expert", None, "batch"),
        P("expert", "batch"),
        P("expert", "batch", None),
        P("expert", None),
    )
    return jax.shard_map(local, mesh=mesh, in_specs=in_specs, out_specs=out_specs, check_vma=False)
```

```python
import functools

import jax
import jax.numpy as jnp
from jax import lax
from jax.experimental import pallas as pl
from jax.experimental.pallas import tpu as pltpu
from jax.sharding import PartitionSpec as P

epsilon = 1e-05
root_half = 0.7071067811865476
gauss_norm = 0.3989422804014327


def gelu_parts(pre_act):
    gelu_value = jax.nn.gelu(pre_act, approximate=False)
    gelu_slope = (
        0.5 * (1.0 + lax.erf(pre_act * root_half))
        + pre_act * jnp.exp(-0.5 * pre_act * pre_act) * gauss_norm
    )
    return (gelu_value.astype(jnp.bfloat16), gelu_slope)


def contract_first(left, right):
    return lax.dot_general(
        left, right, (((0,), (0,)), ((), ())), preferred_element_type=jnp.float32
    )


def contract_last(left, right):
    return lax.dot_general(
        left, right, (((1,), (1,)), ((), ())), preferred_element_type=jnp.float32
    )


def local_general(tokens, routes, centroid, ln_gain, ln_bias, w_in, b_in, w_out, b_out, cotangent):
    experts = lax.axis_size("expert")
    tok_count = tokens.shape[0]
    model_width = tokens.shape[1]
    capacity = max(2, 2 * tok_count // experts)
    row_count = experts * capacity
    route_ids = routes[:, 0]
    onehot = (route_ids[:, None] == jnp.arange(experts, dtype=jnp.int32)[None, :]).astype(jnp.int32)
    before = jnp.cumsum(onehot, axis=0) - onehot
    rank_in = jnp.sum(before * onehot, axis=1)
    target = route_ids * capacity + rank_in
    placing = (jnp.arange(row_count, dtype=jnp.int32)[:, None] == target[None, :]).astype(
        jnp.bfloat16
    )
    outgoing = jnp.dot(placing, tokens, preferred_element_type=jnp.float32).astype(jnp.bfloat16)
    arrived = lax.all_to_all(
        outgoing.reshape(experts, capacity, model_width),
        "expert",
        split_axis=0,
        concat_axis=0,
        tiled=True,
    )
    arrived = arrived.reshape(row_count, model_width)
    hidden_in = arrived.astype(jnp.float32)
    center = jnp.mean(hidden_in, axis=1, keepdims=True)
    spread = jnp.mean((hidden_in - center) * (hidden_in - center), axis=1, keepdims=True)
    inv_std = lax.rsqrt(spread + epsilon)
    normed = (hidden_in - center) * inv_std
    gain_row = ln_gain[0].astype(jnp.float32)
    shift_row = ln_bias[0].astype(jnp.float32)
    cent_row = centroid[0].astype(jnp.float32)
    b_last = b_out[0].astype(jnp.float32)
    lowered = (normed * gain_row + shift_row).astype(jnp.bfloat16)
    gate_logit = jnp.dot(arrived, centroid[0], preferred_element_type=jnp.float32)
    mixing = jax.nn.sigmoid(gate_logit)
    w_first = w_in[0]
    w_second = w_out[0]
    b_first = b_in[0].astype(jnp.float32)
    inputs_all = lax.all_gather(lowered, "batch", axis=0, tiled=True)
    row_piece = inputs_all
    piece_act, unused = gelu_parts(
        jnp.dot(row_piece, w_first, preferred_element_type=jnp.float32) + b_first
    )
    branch = (
        lax.psum_scatter(
            jnp.dot(piece_act, w_second, preferred_element_type=jnp.float32).astype(jnp.bfloat16),
            "batch",
            scatter_dimension=0,
            tiled=True,
        ).astype(jnp.float32)
        + b_last
    )
    expert_out = hidden_in + branch
    reply_rows = (mixing[:, None] * expert_out).astype(jnp.bfloat16)
    returned = lax.all_to_all(
        reply_rows.reshape(experts, capacity, model_width),
        "expert",
        split_axis=0,
        concat_axis=0,
        tiled=True,
    )
    returned = returned.reshape(row_count, model_width)
    mixed = (tokens.astype(jnp.float32) + contract_first(placing, returned)).astype(jnp.bfloat16)
    grad_out = jnp.dot(placing, cotangent, preferred_element_type=jnp.float32).astype(jnp.bfloat16)
    grad_rows = lax.all_to_all(
        grad_out.reshape(experts, capacity, model_width),
        "expert",
        split_axis=0,
        concat_axis=0,
        tiled=True,
    )
    grad_rows = grad_rows.reshape(row_count, model_width).astype(jnp.float32)
    gate_grad = jnp.sum(grad_rows * expert_out, axis=1) * mixing * (1.0 - mixing)
    direct = grad_rows * mixing[:, None]
    branch_grad = direct.astype(jnp.bfloat16)
    b_out_part = jnp.sum(branch_grad.astype(jnp.float32), axis=0)
    centroid_part = jnp.sum(gate_grad[:, None] * hidden_in, axis=0)
    grads_all = lax.all_gather(branch_grad, "batch", axis=0, tiled=True)
    activated, gelu_slope = gelu_parts(
        jnp.dot(inputs_all, w_first, preferred_element_type=jnp.float32) + b_first
    )
    pre_grad = (contract_last(grads_all, w_second) * gelu_slope).astype(jnp.bfloat16)
    w_out_grad = contract_first(activated, grads_all)
    w_in_grad = contract_first(inputs_all, pre_grad)
    b_in_grad = jnp.sum(pre_grad.astype(jnp.float32), axis=0)
    row_piece = pre_grad
    normed_grad = lax.psum_scatter(
        contract_last(row_piece, w_first), "batch", scatter_dimension=0, tiled=True
    )
    gain_part = jnp.sum(normed_grad * normed, axis=0)
    bias_part = jnp.sum(normed_grad, axis=0)
    scaled = normed_grad * gain_row
    ln_grad = inv_std * (
        scaled
        - jnp.mean(scaled, axis=1, keepdims=True)
        - normed * jnp.mean(scaled * normed, axis=1, keepdims=True)
    )
    input_grad = direct + gate_grad[:, None] * cent_row + ln_grad
    outgoing_grads = input_grad.astype(jnp.bfloat16).reshape(experts, capacity, model_width)
    arrived_grads = lax.all_to_all(
        outgoing_grads, "expert", split_axis=0, concat_axis=0, tiled=True
    ).reshape(row_count, model_width)
    tokens_grad = cotangent.astype(jnp.float32) + contract_first(placing, arrived_grads)
    small_sums = lax.psum((centroid_part, gain_part, bias_part, b_out_part), "batch")
    return (
        mixed,
        tokens_grad,
        small_sums[0][None],
        small_sums[1][None],
        small_sums[2][None],
        w_in_grad[None],
        b_in_grad[None],
        w_out_grad[None],
        small_sums[3][None],
    )


f32 = jnp.float32
bf16 = jnp.bfloat16

erfc_step = 0.3 * root_half
erfc_half = tuple(
    0.5 * c
    for c in (
        0.16918935705144628,
        0.1706908732382945,
        0.14852168107322075,
        0.21417961390291307,
        -0.09282143256694776,
        0.5449597059025907,
        -0.5097655323576785,
        0.48429815524087755,
        -0.12925243016104992,
    )
)


def gelu_and_slope(a):
    bell = jnp.exp(-0.5 * a * a)
    t = 1.0 / (1.0 + erfc_step * jnp.abs(a))
    poly = erfc_half[-1]
    for c in erfc_half[-2::-1]:
        poly = poly * t + c
    tail = poly * t * bell
    below = jnp.where(a < 0.0, tail, 1.0 - tail)
    return a * below, below + a * bell * gauss_norm


def whole():
    return pl.BlockSpec(memory_space=pltpu.VMEM)


def call(body, outs, args, name, scratch=(), scalars=0, far=0, limit=12 << 20, after=()):
    count, extra = len(args), len(after)
    args = tuple(
        pltpu.with_memory_space_constraint(x, pltpu.HBM) if scalars <= i < scalars + far else x
        for i, x in enumerate(args)
    )

    def run(*refs):
        body(*refs[:count], *refs[count + extra :])

    return pl.pallas_call(
        run,
        out_shape=tuple(outs),
        in_specs=[pl.BlockSpec(memory_space=pltpu.SMEM)] * scalars
        + [pl.BlockSpec(memory_space=pltpu.HBM)] * far
        + [whole()] * (count - scalars - far)
        + [pl.BlockSpec(memory_space=pl.ANY)] * extra,
        out_specs=tuple(whole() for _ in outs),
        scratch_shapes=list(scratch),
        compiler_params=pltpu.CompilerParams(vmem_limit_bytes=limit),
        cost_estimate=pl.CostEstimate(flops=0, bytes_accessed=0, transcendentals=0),
        name=name,
    )(*args, *after)


def out(rows, cols, dtype):
    return jax.ShapeDtypeStruct((rows, cols), dtype)


def iota(shape, dim):
    return lax.broadcasted_iota(jnp.int32, shape, dim)


def slot_row(capacity, me, row):
    n = row.shape[1]
    wide = jnp.broadcast_to(row, (n, n))
    i, j = iota((n, n), 0), iota((n, n), 1)
    col = jnp.sum(jnp.where(i == j, wide, 0), axis=1, keepdims=True)
    rank = jnp.sum(((col == wide) & (i < j)).astype(jnp.int32), axis=0, keepdims=True)
    return jnp.bitwise_xor(row, me) * capacity + rank


def slot_col(capacity, me, row):
    n = row.shape[1]
    wide = jnp.broadcast_to(row, (n, n))
    i, j = iota((n, n), 0), iota((n, n), 1)
    col = jnp.sum(jnp.where(i == j, wide, 0), axis=1, keepdims=True)
    rank = jnp.sum(((col == wide) & (j < i)).astype(jnp.int32), axis=1, keepdims=True)
    return jnp.bitwise_xor(col, me) * capacity + rank


def dispatch_body(capacity, experts, me, *refs):
    far, parts, rest = refs[:10], refs[10 : 10 + experts], refs[10 + experts :]
    weights, params, tokens, cotangent, routes, sems, *lines = rest
    rows_in, rows_out = far[3].shape[0], far[4].shape[0]
    places = [
        routes,
        tokens,
        cotangent,
        weights.at[0:rows_in],
        weights.at[rows_in : rows_in + rows_out],
        *lines,
    ]
    copies = [
        pltpu.make_async_copy(x, place, sems.at[i])
        for i, (x, place) in enumerate(zip(far, places))
    ]
    for copy in copies:
        copy.start()
    slots = experts * capacity
    copies[0].wait()
    n = routes.shape[1]
    slot = slot_row(capacity, me[0], routes[...])
    place = (iota((slots, n), 0) == jnp.broadcast_to(slot, (slots, n))).astype(bf16)
    copies[1].wait()
    rows = jnp.dot(place, tokens[...], preferred_element_type=f32).astype(bf16)
    for d, part in enumerate(parts):
        part[0:capacity, :] = rows[d * capacity : (d + 1) * capacity, :]
    copies[2].wait()
    grads = jnp.dot(place, cotangent[...], preferred_element_type=f32).astype(bf16)
    for d, part in enumerate(parts):
        part[capacity:, :] = grads[d * capacity : (d + 1) * capacity, :]
    for copy in copies[3:]:
        copy.wait()
    spare = weights.shape[0] - rows_in - rows_out
    weights[rows_in + rows_out :, :] = jnp.broadcast_to(lines[0][...], (spare, lines[0].shape[1]))
    for i, line in enumerate(lines[1:]):
        params[i : i + 1, :] = line[...].astype(f32)
    params[len(lines) - 1 :, :] = jnp.zeros_like(params[len(lines) - 1 :, :])


def row_mean(x):
    return jnp.mean(x, axis=1, keepdims=True)


def norm_parts(h):
    center = row_mean(h)
    spread = row_mean((h - center) * (h - center))
    inv_std = lax.rsqrt(spread + epsilon)
    return (h - center) * inv_std, inv_std


def gate(h, cent):
    return jax.nn.sigmoid(jnp.sum(h * cent, axis=1, keepdims=True))


def enter_body(capacity, count, *refs):
    parts, (params, both) = refs[:count], refs[count:]
    cent, gain, shift = (params[i : i + 1, :] for i in range(3))
    half = count * capacity
    for j, part in enumerate(parts):
        h = part[0:capacity, :].astype(f32)
        normed, unused = norm_parts(h)
        lowered = normed * gain + shift
        at = j * capacity
        both[at : at + capacity, :] = lowered.astype(bf16)
        mixing = gate(h, cent)
        both[half + at : half + at + capacity, :] = (
            part[capacity:, :].astype(f32) * mixing
        ).astype(bf16)


def middle_body(count, half, first, *refs):
    own, other, refs = refs[:count], refs[count : 2 * count], refs[2 * count :]
    quarters, refs = refs[:2], refs[2:]
    if not first:
        before, refs = refs[0], refs[1:]
    keep, send, n_all, dz_all, u0, da0, u1, da1, sums, z_acc, dn_acc = refs
    at = 0
    for both in own + other:
        rows = both.shape[0] // 2
        n_all[at : at + rows, :] = both[0:rows, :]
        dz_all[at : at + rows, :] = both[rows:, :]
        at += rows
    width, hidden = n_all.shape[1], u0.shape[1]
    for q, (weights, u_ref, da_ref) in enumerate(
        ((quarters[0], u0, da0), (quarters[1], u1, da1))
    ):
        wi, wo = weights.at[0:width], weights.at[width : width + hidden]
        b = weights.at[width + hidden : width + hidden + 1]
        a = jnp.dot(n_all[...], wi[...], preferred_element_type=f32) + b[...].astype(f32)
        t = contract_last(dz_all[...], wo[...])
        u, slope = gelu_and_slope(a)
        u = u.astype(bf16)
        u_ref[...] = u
        z = jnp.dot(u, wo[...], preferred_element_type=f32)
        da = (t * slope).astype(bf16)
        da_ref[...] = da
        dn = contract_last(da, wi[...])
        total = jnp.sum(da.astype(f32), axis=0, keepdims=True)
        if not first:
            total = total + before[q : q + 1, :]
        sums[q : q + 1, :] = total
        if q == 0:
            z_acc[...] = z
            dn_acc[...] = dn
        else:
            z_acc[...] += z
            dn_acc[...] += dn
    sums[2:, :] = jnp.zeros_like(sums[2:, :])
    keep[0:half, :] = z_acc[0:half, :]
    keep[half:, :] = dn_acc[0:half, :]
    send[0:half, :] = z_acc[half:, :].astype(bf16)
    send[half:, :] = dn_acc[half:, :].astype(bf16)


def leave_body(capacity, count, first, last, *refs):
    parts, refs = refs[:count], refs[count:]
    (keep, came, params), refs = refs[:3], refs[3:]
    if not first:
        before, refs = refs[0], refs[1:]
    if last:
        hidden_sums, refs = refs[0], refs[1:]
    replies, sums = refs[:count], refs[count]
    half = count * capacity
    cent_row, gain_row, last_row = (params[i : i + 1, :] for i in (0, 1, 3))
    totals = [0.0, 0.0, 0.0, 0.0]
    for j, part in enumerate(parts):
        at = j * capacity
        h = part[0:capacity, :].astype(f32)
        g = part[capacity:, :].astype(f32)
        z = keep[at : at + capacity, :] + came[at : at + capacity, :].astype(f32)
        dn = (
            keep[half + at : half + at + capacity, :]
            + came[half + at : half + at + capacity, :].astype(f32)
        )
        f = h + (z + last_row)
        mixing = gate(h, cent_row)
        replies[j][0:capacity, :] = (mixing * f).astype(bf16)
        p = jnp.sum(g * f, axis=1, keepdims=True) * mixing * (1.0 - mixing)
        direct = g * mixing
        normed, inv_std = norm_parts(h)
        w = dn * gain_row
        dh = (
            direct
            + p * cent_row
            + inv_std * (w - row_mean(w) - normed * row_mean(w * normed))
        )
        replies[j][capacity:, :] = dh.astype(bf16)
        for i, rows in enumerate((p * h, dn * normed, dn, direct.astype(bf16).astype(f32))):
            totals[i] = totals[i] + jnp.sum(rows, axis=0, keepdims=True)
    for i, total in enumerate(totals):
        if not first:
            total = total + before[i : i + 1, :]
        sums[i : i + 1, :] = total
    if last:
        sums[4:6, :] = hidden_sums[0:2, :]
        sums[6:, :] = jnp.zeros_like(sums[6:, :])
    else:
        sums[4:, :] = jnp.zeros_like(sums[4:, :])


def weights_body(chunks, *refs):
    u, da, n, dz = (refs[i * chunks : (i + 1) * chunks] for i in range(4))
    rest = refs[4 * chunks :]
    width, hidden = n[0].shape[1], u[0].shape[1]
    step = 512
    for k, (left, right) in enumerate(((n, da), (u, dz))):
        size = left[0].shape[1]
        grad, offset = (rest[0], k * width) if len(rest) == 1 else (rest[1 + k], 0)

        def some(i, unused, left=left, right=right, grad=grad, offset=offset, k=k):
            at = pl.multiple_of(i * step, step)
            total = contract_first(
                jnp.concatenate([x[:, pl.ds(at, step)] for x in left], axis=0),
                jnp.concatenate([x[...] for x in right], axis=0),
            )
            if len(rest) == 3:
                total = total + rest[0][pl.ds(k * width + at, step), :].astype(f32)
            grad[pl.ds(offset + at, step), :] = total.astype(grad.dtype)
            return unused

        lax.fori_loop(0, size // step, some, 0)


def combine_body(capacity, me, routes, tokens, cotangent, *refs):
    replies, (mixed, tokens_grad) = refs[:-2], refs[-2:]
    slots = len(replies) * capacity
    n = routes.shape[1]
    slot = slot_col(capacity, me[0], routes[...])
    place = (iota((n, slots), 1) == jnp.broadcast_to(slot, (n, slots))).astype(bf16)
    rows = jnp.concatenate([x[0:capacity, :] for x in replies], axis=0)
    grads = jnp.concatenate([x[capacity:, :] for x in replies], axis=0)
    mixed[...] = (
        tokens[...].astype(f32) + jnp.dot(place, rows, preferred_element_type=f32)
    ).astype(bf16)
    tokens_grad[...] = cotangent[...].astype(f32) + jnp.dot(
        place, grads, preferred_element_type=f32
    )


class Order:
    def __init__(self):
        self.fence = []

    def kernel(self, body, outs, args, name, **more):
        mine = {id(x) for x in args}
        after = [x for x in self.fence if id(x) not in mine]
        got = call(body, outs, args, name, after=after, **more)
        self.fence = [got[-1]]
        return got

    def start(self, x, axis, offset, name="rows"):
        others = [y for y in self.fence if y is not x]
        if others:
            x = lax.optimization_barrier((x, *others))[0]
        size = lax.axis_size(axis)
        with jax.named_scope(name):
            return lax.ppermute(x, axis, [(i, i ^ offset) for i in range(size)])

    def wait(self, *arrays):
        self.fence = self.fence + list(arrays)


def local_paired(tokens, routes, centroid, ln_gain, ln_bias, w_in, b_in, w_out, b_out, cotangent):
    experts = lax.axis_size("expert")
    tok_count, width = tokens.shape
    capacity = 2 * tok_count // experts
    hidden = w_in.shape[2]
    core, chip = 1, 2
    order = Order()
    me = lax.axis_index("expert").astype(jnp.int32).reshape(1)
    *parts, weights, params, tokens_near, cotangent_near, routes_near = order.kernel(
        functools.partial(dispatch_body, capacity, experts),
        [out(2 * capacity, width, bf16)] * experts
        + [
            out(width + hidden + 16, hidden, bf16),
            out(8, width, f32),
            out(tok_count, width, bf16),
            out(tok_count, width, bf16),
            out(1, tok_count, jnp.int32),
        ],
        (
            *(me, routes.reshape(1, tok_count), tokens, cotangent, w_in[0], w_out[0], b_in),
            *(centroid, ln_gain, ln_bias, b_out),
        ),
        "dispatch",
        scalars=1,
        far=10,
        scratch=[pltpu.SemaphoreType.DMA((10,))]
        + [pltpu.VMEM((1, x.shape[1]), bf16) for x in (b_in, centroid, ln_gain, ln_bias, b_out)],
    )
    order.fence = [params]
    arrived = {0: parts[0]}
    both, other, mids, replies, left = {}, {}, {}, {}, {}
    sums = {"middle": (), "leave": ()}

    def send(*ds):
        for d in ds:
            arrived[d] = order.start(parts[d], "expert", d, f"out_{d}")

    def sent(*ds):
        order.wait(*[arrived[d] for d in ds])

    def enter(c, ds):
        both[c] = order.kernel(
            functools.partial(enter_body, capacity, len(ds)),
            [out(2 * len(ds) * capacity, width, bf16)],
            (*[arrived[d] for d in ds], params),
            "enter",
        )[0]
        other[c] = order.start(both[c], "batch", chip, f"share_{c}")

    def middle(c, cs):
        half = sum(both[i].shape[0] for i in cs) // 2
        mids[c] = order.kernel(
            functools.partial(middle_body, len(cs), half, not sums["middle"]),
            [out(2 * half, width, f32), out(2 * half, width, bf16)]
            + [out(2 * half, width, bf16)] * 2
            + [out(2 * half, hidden, bf16)] * 4
            + [out(8, hidden, f32)],
            (
                *[both[i] for i in cs],
                *[other[i] for i in cs],
                *(weights, sibling),
                *sums["middle"],
            ),
            "middle",
            scratch=[pltpu.VMEM((2 * half, width), f32)] * 2,
            limit=24 << 20,
        )
        sums["middle"] = (mids[c][8],)
        left[c] = order.start(mids[c][1], "batch", chip, f"sums_{c}")

    def leave(c, ds, last=False):
        *gone, total = order.kernel(
            functools.partial(leave_body, capacity, len(ds), not sums["leave"], last),
            [out(2 * capacity, width, bf16)] * len(ds) + [out(8, width, f32)],
            (
                *[arrived[d] for d in ds],
                *(mids[c][0], left[c], params),
                *sums["leave"],
                *(sums["middle"] if last else ()),
            ),
            "leave",
        )
        sums["leave"] = (total,)
        for d, x in zip(ds, gone):
            replies[d] = x

    def reply(*ds):
        for d in ds:
            replies[d] = order.start(replies[d], "expert", d, f"reply_{d}")

    def replied(*ds):
        order.wait(*[replies[d] for d in ds])

    per = max(1, 128 // capacity)
    near, z1, z2, z3 = (list(range(d, d + per)) for d in range(0, experts, per))
    enter("0a", near[:1])
    send(*z3)
    send(*near[1:])
    sibling = order.start(weights, "batch", core, "weights")
    sent(*near[1:])
    enter("0b", near[1:])
    order.wait(other["0a"])
    send(z1[0])
    order.wait(sibling)
    send(z1[1])
    order.wait(other["0b"])
    middle(0, ["0a", "0b"])
    sent(*z1)
    enter(1, z1)
    sent(*z3)
    send(*z2)
    enter(3, z3)
    order.wait(left[0])
    leave(0, near)
    reply(*near[1:])
    order.wait(other[1])
    middle(1, [1])
    order.wait(other[3])
    middle(3, [3])
    replied(*near[1:])
    sent(*z2)
    enter(2, z2)
    order.wait(left[1])
    leave(1, z1)
    reply(*z1)
    order.wait(other[2])
    middle(2, [2])
    order.wait(left[3])
    leave(3, z3)
    reply(*z3)
    own = [mids[c] for c in mids]

    def pick(*which):
        return [x[i] for i in which for x in own]

    (shares,) = order.kernel(
        functools.partial(weights_body, len(own)),
        [out(width + hidden, hidden, bf16)],
        pick(6, 7, 2, 3),
        "sibling_weights",
    )
    replied(*z1)
    shares = order.start(shares, "batch", core, "grads")
    order.wait(left[2])
    leave(2, z2, last=True)
    order.wait(shares)
    reply(*z2)
    total = sums["leave"][0]
    total_core = order.start(total, "batch", core, "total")
    order.wait(total_core)
    b_in_grad = total[4:5] + total_core[5:6]
    total = total + total_core
    total_chip = order.start(total, "batch", chip, "total")
    replied(*z3)
    w_in_grad, w_out_grad = order.kernel(
        functools.partial(weights_body, len(own)),
        [out(width, hidden, f32), out(hidden, width, f32)],
        (*pick(4, 5, 2, 3), shares),
        "own_weights",
    )
    total = total + total_chip
    mixed, tokens_grad = order.kernel(
        functools.partial(combine_body, capacity),
        [out(tok_count, width, bf16), out(tok_count, width, f32)],
        (me, routes_near, tokens_near, cotangent_near, *[replies[d] for d in range(experts)]),
        "combine",
        scalars=1,
    )
    return (
        mixed,
        tokens_grad,
        total[0:1],
        total[1:2],
        total[2:3],
        w_in_grad[None],
        b_in_grad,
        w_out_grad[None],
        total[3:4],
    )


def local(tokens, routes, centroid, ln_gain, ln_bias, w_in, b_in, w_out, b_out, cotangent):
    experts = lax.axis_size("expert")
    tok_count, width = tokens.shape
    capacity = 2 * tok_count // experts
    power_of_two = experts & (experts - 1) == 0
    paired = (
        lax.axis_size("batch") == 4
        and power_of_two
        and capacity % 16 == 0
        and capacity <= 128
        and width == w_in.shape[2]
        and width % 128 == 0
    )
    plan = local_paired if paired else local_general
    return plan(
        tokens, routes, centroid, ln_gain, ln_bias, w_in, b_in, w_out, b_out, cotangent
    )


def solution(mesh):
    in_specs = (
        P(("expert", "batch"), None),
        P(("expert", "batch"), None),
        P("expert", None),
        P("expert", None),
        P("expert", None),
        P("expert", None, "batch"),
        P("expert", "batch"),
        P("expert", "batch", None),
        P("expert", None),
        P(("expert", "batch"), None),
    )
    out_specs = (
        P(("expert", "batch"), None),
        P(("expert", "batch"), None),
        P("expert", None),
        P("expert", None),
        P("expert", None),
        P("expert", None, "batch"),
        P("expert", "batch"),
        P("expert", "batch", None),
        P("expert", None),
    )
    return jax.shard_map(local, mesh=mesh, in_specs=in_specs, out_specs=out_specs, check_vma=False)
```

```python
import functools

import jax
import jax.numpy as jnp
from jax import lax
from jax.experimental import pallas as pl
from jax.experimental.pallas import tpu as pltpu
from jax.sharding import PartitionSpec as P

epsilon = 1e-05
root_half = 0.7071067811865476
gauss_norm = 0.3989422804014327


def gelu_parts(pre_act):
    gelu_value = jax.nn.gelu(pre_act, approximate=False)
    gelu_slope = (
        0.5 * (1.0 + lax.erf(pre_act * root_half))
        + pre_act * jnp.exp(-0.5 * pre_act * pre_act) * gauss_norm
    )
    return (gelu_value.astype(jnp.bfloat16), gelu_slope)


def contract_first(left, right):
    return lax.dot_general(
        left, right, (((0,), (0,)), ((), ())), preferred_element_type=jnp.float32
    )


def contract_last(left, right):
    return lax.dot_general(
        left, right, (((1,), (1,)), ((), ())), preferred_element_type=jnp.float32
    )


def local_general(tokens, routes, centroid, ln_gain, ln_bias, w_in, b_in, w_out, b_out, cotangent):
    experts = lax.axis_size("expert")
    tok_count = tokens.shape[0]
    model_width = tokens.shape[1]
    capacity = max(2, 2 * tok_count // experts)
    row_count = experts * capacity
    route_ids = routes[:, 0]
    onehot = (route_ids[:, None] == jnp.arange(experts, dtype=jnp.int32)[None, :]).astype(jnp.int32)
    before = jnp.cumsum(onehot, axis=0) - onehot
    rank_in = jnp.sum(before * onehot, axis=1)
    target = route_ids * capacity + rank_in
    placing = (jnp.arange(row_count, dtype=jnp.int32)[:, None] == target[None, :]).astype(
        jnp.bfloat16
    )
    outgoing = jnp.dot(placing, tokens, preferred_element_type=jnp.float32).astype(jnp.bfloat16)
    arrived = lax.all_to_all(
        outgoing.reshape(experts, capacity, model_width),
        "expert",
        split_axis=0,
        concat_axis=0,
        tiled=True,
    )
    arrived = arrived.reshape(row_count, model_width)
    hidden_in = arrived.astype(jnp.float32)
    center = jnp.mean(hidden_in, axis=1, keepdims=True)
    spread = jnp.mean((hidden_in - center) * (hidden_in - center), axis=1, keepdims=True)
    inv_std = lax.rsqrt(spread + epsilon)
    normed = (hidden_in - center) * inv_std
    gain_row = ln_gain[0].astype(jnp.float32)
    shift_row = ln_bias[0].astype(jnp.float32)
    cent_row = centroid[0].astype(jnp.float32)
    b_last = b_out[0].astype(jnp.float32)
    lowered = (normed * gain_row + shift_row).astype(jnp.bfloat16)
    gate_logit = jnp.dot(arrived, centroid[0], preferred_element_type=jnp.float32)
    mixing = jax.nn.sigmoid(gate_logit)
    w_first = w_in[0]
    w_second = w_out[0]
    b_first = b_in[0].astype(jnp.float32)
    inputs_all = lax.all_gather(lowered, "batch", axis=0, tiled=True)
    row_piece = inputs_all
    piece_act, unused = gelu_parts(
        jnp.dot(row_piece, w_first, preferred_element_type=jnp.float32) + b_first
    )
    branch = (
        lax.psum_scatter(
            jnp.dot(piece_act, w_second, preferred_element_type=jnp.float32).astype(jnp.bfloat16),
            "batch",
            scatter_dimension=0,
            tiled=True,
        ).astype(jnp.float32)
        + b_last
    )
    expert_out = hidden_in + branch
    reply_rows = (mixing[:, None] * expert_out).astype(jnp.bfloat16)
    returned = lax.all_to_all(
        reply_rows.reshape(experts, capacity, model_width),
        "expert",
        split_axis=0,
        concat_axis=0,
        tiled=True,
    )
    returned = returned.reshape(row_count, model_width)
    mixed = (tokens.astype(jnp.float32) + contract_first(placing, returned)).astype(jnp.bfloat16)
    grad_out = jnp.dot(placing, cotangent, preferred_element_type=jnp.float32).astype(jnp.bfloat16)
    grad_rows = lax.all_to_all(
        grad_out.reshape(experts, capacity, model_width),
        "expert",
        split_axis=0,
        concat_axis=0,
        tiled=True,
    )
    grad_rows = grad_rows.reshape(row_count, model_width).astype(jnp.float32)
    gate_grad = jnp.sum(grad_rows * expert_out, axis=1) * mixing * (1.0 - mixing)
    direct = grad_rows * mixing[:, None]
    branch_grad = direct.astype(jnp.bfloat16)
    b_out_part = jnp.sum(branch_grad.astype(jnp.float32), axis=0)
    centroid_part = jnp.sum(gate_grad[:, None] * hidden_in, axis=0)
    grads_all = lax.all_gather(branch_grad, "batch", axis=0, tiled=True)
    activated, gelu_slope = gelu_parts(
        jnp.dot(inputs_all, w_first, preferred_element_type=jnp.float32) + b_first
    )
    pre_grad = (contract_last(grads_all, w_second) * gelu_slope).astype(jnp.bfloat16)
    w_out_grad = contract_first(activated, grads_all)
    w_in_grad = contract_first(inputs_all, pre_grad)
    b_in_grad = jnp.sum(pre_grad.astype(jnp.float32), axis=0)
    row_piece = pre_grad
    normed_grad = lax.psum_scatter(
        contract_last(row_piece, w_first), "batch", scatter_dimension=0, tiled=True
    )
    gain_part = jnp.sum(normed_grad * normed, axis=0)
    bias_part = jnp.sum(normed_grad, axis=0)
    scaled = normed_grad * gain_row
    ln_grad = inv_std * (
        scaled
        - jnp.mean(scaled, axis=1, keepdims=True)
        - normed * jnp.mean(scaled * normed, axis=1, keepdims=True)
    )
    input_grad = direct + gate_grad[:, None] * cent_row + ln_grad
    outgoing_grads = input_grad.astype(jnp.bfloat16).reshape(experts, capacity, model_width)
    arrived_grads = lax.all_to_all(
        outgoing_grads, "expert", split_axis=0, concat_axis=0, tiled=True
    ).reshape(row_count, model_width)
    tokens_grad = cotangent.astype(jnp.float32) + contract_first(placing, arrived_grads)
    small_sums = lax.psum((centroid_part, gain_part, bias_part, b_out_part), "batch")
    return (
        mixed,
        tokens_grad,
        small_sums[0][None],
        small_sums[1][None],
        small_sums[2][None],
        w_in_grad[None],
        b_in_grad[None],
        w_out_grad[None],
        small_sums[3][None],
    )


f32 = jnp.float32
bf16 = jnp.bfloat16

erfc_step = 0.3 * root_half
erfc_half = tuple(
    0.5 * c
    for c in (
        0.16918935705144628,
        0.1706908732382945,
        0.14852168107322075,
        0.21417961390291307,
        -0.09282143256694776,
        0.5449597059025907,
        -0.5097655323576785,
        0.48429815524087755,
        -0.12925243016104992,
    )
)


def gelu_and_slope(a):
    bell = jnp.exp(-0.5 * a * a)
    t = 1.0 / (1.0 + erfc_step * jnp.abs(a))
    poly = erfc_half[-1]
    for c in erfc_half[-2::-1]:
        poly = poly * t + c
    tail = poly * t * bell
    below = jnp.where(a < 0.0, tail, 1.0 - tail)
    return a * below, below + a * bell * gauss_norm


def whole():
    return pl.BlockSpec(memory_space=pltpu.VMEM)


def call(body, outs, args, name, scratch=(), scalars=0, far=0, limit=12 << 20, after=()):
    count, extra = len(args), len(after)
    args = tuple(
        pltpu.with_memory_space_constraint(x, pltpu.HBM) if scalars <= i < scalars + far else x
        for i, x in enumerate(args)
    )

    def run(*refs):
        body(*refs[:count], *refs[count + extra :])

    return pl.pallas_call(
        run,
        out_shape=tuple(outs),
        in_specs=[pl.BlockSpec(memory_space=pltpu.SMEM)] * scalars
        + [pl.BlockSpec(memory_space=pltpu.HBM)] * far
        + [whole()] * (count - scalars - far)
        + [pl.BlockSpec(memory_space=pl.ANY)] * extra,
        out_specs=tuple(whole() for _ in outs),
        scratch_shapes=list(scratch),
        compiler_params=pltpu.CompilerParams(vmem_limit_bytes=limit),
        cost_estimate=pl.CostEstimate(flops=0, bytes_accessed=0, transcendentals=0),
        name=name,
    )(*args, *after)


def out(rows, cols, dtype):
    return jax.ShapeDtypeStruct((rows, cols), dtype)


def iota(shape, dim):
    return lax.broadcasted_iota(jnp.int32, shape, dim)


def slot_row(capacity, me, row):
    n = row.shape[1]
    wide = jnp.broadcast_to(row, (n, n))
    i, j = iota((n, n), 0), iota((n, n), 1)
    col = jnp.sum(jnp.where(i == j, wide, 0), axis=1, keepdims=True)
    rank = jnp.sum(((col == wide) & (i < j)).astype(jnp.int32), axis=0, keepdims=True)
    return jnp.bitwise_xor(row, me) * capacity + rank


def slot_col(capacity, me, row):
    n = row.shape[1]
    wide = jnp.broadcast_to(row, (n, n))
    i, j = iota((n, n), 0), iota((n, n), 1)
    col = jnp.sum(jnp.where(i == j, wide, 0), axis=1, keepdims=True)
    rank = jnp.sum(((col == wide) & (j < i)).astype(jnp.int32), axis=1, keepdims=True)
    return jnp.bitwise_xor(col, me) * capacity + rank


def dispatch_body(capacity, experts, me, *refs):
    far, parts, rest = refs[:10], refs[10 : 10 + experts], refs[10 + experts :]
    weights, params, tokens, cotangent, routes, sems, *lines = rest
    rows_in, rows_out = far[3].shape[0], far[4].shape[0]
    places = [
        routes,
        tokens,
        cotangent,
        weights.at[0:rows_in],
        weights.at[rows_in : rows_in + rows_out],
        *lines,
    ]
    copies = [
        pltpu.make_async_copy(x, place, sems.at[i])
        for i, (x, place) in enumerate(zip(far, places))
    ]
    for copy in copies:
        copy.start()
    slots = experts * capacity
    copies[0].wait()
    n = routes.shape[1]
    slot = slot_row(capacity, me[0], routes[...])
    place = (iota((slots, n), 0) == jnp.broadcast_to(slot, (slots, n))).astype(bf16)
    copies[1].wait()
    rows = jnp.dot(place, tokens[...], preferred_element_type=f32).astype(bf16)
    for d, part in enumerate(parts):
        part[0:capacity, :] = rows[d * capacity : (d + 1) * capacity, :]
    copies[2].wait()
    grads = jnp.dot(place, cotangent[...], preferred_element_type=f32).astype(bf16)
    for d, part in enumerate(parts):
        part[capacity:, :] = grads[d * capacity : (d + 1) * capacity, :]
    for copy in copies[3:]:
        copy.wait()
    spare = weights.shape[0] - rows_in - rows_out
    weights[rows_in + rows_out :, :] = jnp.broadcast_to(lines[0][...], (spare, lines[0].shape[1]))
    for i, line in enumerate(lines[1:]):
        params[i : i + 1, :] = line[...].astype(f32)
    params[len(lines) - 1 :, :] = jnp.zeros_like(params[len(lines) - 1 :, :])


def row_mean(x):
    return jnp.mean(x, axis=1, keepdims=True)


def norm_parts(h):
    center = row_mean(h)
    spread = row_mean((h - center) * (h - center))
    inv_std = lax.rsqrt(spread + epsilon)
    return (h - center) * inv_std, inv_std


def gate(h, cent):
    return jax.nn.sigmoid(jnp.sum(h * cent, axis=1, keepdims=True))


def enter_body(capacity, count, *refs):
    parts, (params, both) = refs[:count], refs[count:]
    cent, gain, shift = (params[i : i + 1, :] for i in range(3))
    half = count * capacity
    for j, part in enumerate(parts):
        h = part[0:capacity, :].astype(f32)
        normed, unused = norm_parts(h)
        lowered = normed * gain + shift
        at = j * capacity
        both[at : at + capacity, :] = lowered.astype(bf16)
        mixing = gate(h, cent)
        both[half + at : half + at + capacity, :] = (
            part[capacity:, :].astype(f32) * mixing
        ).astype(bf16)


def middle_body(count, half, first, *refs):
    own, other, refs = refs[:count], refs[count : 2 * count], refs[2 * count :]
    quarters, refs = refs[:2], refs[2:]
    if not first:
        before, refs = refs[0], refs[1:]
    keep, send, n_all, dz_all, u0, da0, u1, da1, sums, z_acc, dn_acc = refs
    at = 0
    for both in own + other:
        rows = both.shape[0] // 2
        n_all[at : at + rows, :] = both[0:rows, :]
        dz_all[at : at + rows, :] = both[rows:, :]
        at += rows
    width, hidden = n_all.shape[1], u0.shape[1]
    for q, (weights, u_ref, da_ref) in enumerate(
        ((quarters[0], u0, da0), (quarters[1], u1, da1))
    ):
        wi, wo = weights.at[0:width], weights.at[width : width + hidden]
        b = weights.at[width + hidden : width + hidden + 1]
        a = jnp.dot(n_all[...], wi[...], preferred_element_type=f32) + b[...].astype(f32)
        t = contract_last(dz_all[...], wo[...])
        u, slope = gelu_and_slope(a)
        u = u.astype(bf16)
        u_ref[...] = u
        z = jnp.dot(u, wo[...], preferred_element_type=f32)
        da = (t * slope).astype(bf16)
        da_ref[...] = da
        dn = contract_last(da, wi[...])
        total = jnp.sum(da.astype(f32), axis=0, keepdims=True)
        if not first:
            total = total + before[q : q + 1, :]
        sums[q : q + 1, :] = total
        if q == 0:
            z_acc[...] = z
            dn_acc[...] = dn
        else:
            z_acc[...] += z
            dn_acc[...] += dn
    sums[2:, :] = jnp.zeros_like(sums[2:, :])
    keep[0:half, :] = z_acc[0:half, :]
    keep[half:, :] = dn_acc[0:half, :]
    send[0:half, :] = z_acc[half:, :].astype(bf16)
    send[half:, :] = dn_acc[half:, :].astype(bf16)


def leave_body(capacity, count, first, last, *refs):
    parts, refs = refs[:count], refs[count:]
    (keep, came, params), refs = refs[:3], refs[3:]
    if not first:
        before, refs = refs[0], refs[1:]
    if last:
        hidden_sums, refs = refs[0], refs[1:]
    replies, sums = refs[:count], refs[count]
    half = count * capacity
    cent_row, gain_row, last_row = (params[i : i + 1, :] for i in (0, 1, 3))
    totals = [0.0, 0.0, 0.0, 0.0]
    for j, part in enumerate(parts):
        at = j * capacity
        h = part[0:capacity, :].astype(f32)
        g = part[capacity:, :].astype(f32)
        z = keep[at : at + capacity, :] + came[at : at + capacity, :].astype(f32)
        dn = (
            keep[half + at : half + at + capacity, :]
            + came[half + at : half + at + capacity, :].astype(f32)
        )
        f = h + (z + last_row)
        mixing = gate(h, cent_row)
        replies[j][0:capacity, :] = (mixing * f).astype(bf16)
        p = jnp.sum(g * f, axis=1, keepdims=True) * mixing * (1.0 - mixing)
        direct = g * mixing
        normed, inv_std = norm_parts(h)
        w = dn * gain_row
        dh = (
            direct
            + p * cent_row
            + inv_std * (w - row_mean(w) - normed * row_mean(w * normed))
        )
        replies[j][capacity:, :] = dh.astype(bf16)
        for i, rows in enumerate((p * h, dn * normed, dn, direct.astype(bf16).astype(f32))):
            totals[i] = totals[i] + jnp.sum(rows, axis=0, keepdims=True)
    for i, total in enumerate(totals):
        if not first:
            total = total + before[i : i + 1, :]
        sums[i : i + 1, :] = total
    if last:
        sums[4:6, :] = hidden_sums[0:2, :]
        sums[6:, :] = jnp.zeros_like(sums[6:, :])
    else:
        sums[4:, :] = jnp.zeros_like(sums[4:, :])


def weights_body(chunks, *refs):
    u, da, n, dz = (refs[i * chunks : (i + 1) * chunks] for i in range(4))
    rest = refs[4 * chunks :]
    width, hidden = n[0].shape[1], u[0].shape[1]
    step = 512
    for k, (left, right) in enumerate(((n, da), (u, dz))):
        size = left[0].shape[1]
        grad, offset = (rest[0], k * width) if len(rest) == 1 else (rest[1 + k], 0)

        def some(i, unused, left=left, right=right, grad=grad, offset=offset, k=k):
            at = pl.multiple_of(i * step, step)
            total = contract_first(
                jnp.concatenate([x[:, pl.ds(at, step)] for x in left], axis=0),
                jnp.concatenate([x[...] for x in right], axis=0),
            )
            if len(rest) == 4:
                total = total + rest[0][pl.ds(k * width + at, step), :].astype(f32)
            grad[pl.ds(offset + at, step), :] = total.astype(grad.dtype)
            return unused

        lax.fori_loop(0, size // step, some, 0)
    if len(rest) == 4:
        rest[3][...] = jnp.zeros_like(rest[3])


def combine_body(capacity, me, routes, tokens, cotangent, *refs):
    replies, (mixed, tokens_grad) = refs[:-2], refs[-2:]
    slots = len(replies) * capacity
    n = routes.shape[1]
    slot = slot_col(capacity, me[0], routes[...])
    place = (iota((n, slots), 1) == jnp.broadcast_to(slot, (n, slots))).astype(bf16)
    rows = jnp.concatenate([x[0:capacity, :] for x in replies], axis=0)
    grads = jnp.concatenate([x[capacity:, :] for x in replies], axis=0)
    mixed[...] = (
        tokens[...].astype(f32) + jnp.dot(place, rows, preferred_element_type=f32)
    ).astype(bf16)
    tokens_grad[...] = cotangent[...].astype(f32) + jnp.dot(
        place, grads, preferred_element_type=f32
    )


class Order:
    def __init__(self):
        self.fence = []

    def kernel(self, body, outs, args, name, **more):
        mine = {id(x) for x in args}
        after = [x for x in self.fence if id(x) not in mine]
        got = call(body, outs, args, name, after=after, **more)
        self.fence = [got[-1]]
        return got

    def start(self, x, axis, offset, what, index=None):
        others = [y for y in self.fence if y is not x]
        if others:
            x = lax.optimization_barrier((x, *others))[0]
        size = lax.axis_size(axis)
        with jax.named_scope(f"t{what}_{offset if index is None else index}"):
            return lax.ppermute(x, axis, [(i, i ^ offset) for i in range(size)])

    def wait(self, array):
        self.fence = self.fence + [array]


(
    DISPATCH,
    ENTER,
    MIDDLE,
    LEAVE,
    SIBLING,
    OWN,
    ADD,
    FINISH,
    COMBINE,
    ROWS,
    SHARE,
    SUMS,
    REPLY,
    WEIGHTS,
    GRADS,
    TOTAL,
    BOTH,
    PARAMS,
    NEAR,
    BIAS,
) = range(20)
RUN, SEND, WAIT = range(3)

shares = ((0,), (6,), (1, 5), (2, 4), (3, 7))
chunks = ((0, 1), (2,), (3,), (4,))

plan = (
    (RUN, DISPATCH, 0),
    (SEND, ROWS, 4),
    (SEND, ROWS, 5),
    (SEND, WEIGHTS, 0),
    (SEND, ROWS, 2),
    (RUN, ENTER, 0),
    (SEND, SHARE, 0),
    (WAIT, WEIGHTS, 0),
    (SEND, ROWS, 1),
    (SEND, ROWS, 6),
    (SEND, ROWS, 3),
    (WAIT, ROWS, 4),
    (WAIT, ROWS, 2),
    (RUN, ENTER, 3),
    (SEND, SHARE, 3),
    (SEND, ROWS, 7),
    (WAIT, SHARE, 0),
    (WAIT, ROWS, 1),
    (WAIT, ROWS, 5),
    (RUN, ENTER, 2),
    (SEND, SHARE, 2),
    (WAIT, SHARE, 3),
    (RUN, MIDDLE, 2),
    (SEND, SUMS, 2),
    (WAIT, SHARE, 2),
    (RUN, MIDDLE, 1),
    (SEND, SUMS, 1),
    (WAIT, ROWS, 6),
    (RUN, ENTER, 1),
    (WAIT, ROWS, 3),
    (SEND, SHARE, 1),
    (WAIT, SHARE, 1),
    (WAIT, ROWS, 7),
    (RUN, ENTER, 4),
    (SEND, SHARE, 4),
    (WAIT, SUMS, 2),
    (RUN, LEAVE, 2),
    (SEND, REPLY, 2),
    (SEND, REPLY, 4),
    (WAIT, SUMS, 1),
    (RUN, LEAVE, 1),
    (SEND, REPLY, 5),
    (RUN, MIDDLE, 0),
    (SEND, REPLY, 1),
    (WAIT, REPLY, 4),
    (SEND, SUMS, 0),
    (WAIT, SHARE, 4),
    (RUN, MIDDLE, 3),
    (SEND, SUMS, 3),
    (RUN, SIBLING, 0),
    (WAIT, SUMS, 0),
    (WAIT, REPLY, 5),
    (SEND, GRADS, 0),
    (RUN, LEAVE, 0),
    (SEND, REPLY, 6),
    (WAIT, REPLY, 1),
    (WAIT, REPLY, 2),
    (WAIT, SUMS, 3),
    (RUN, LEAVE, 3),
    (SEND, REPLY, 7),
    (SEND, TOTAL, 0),
    (WAIT, GRADS, 0),
    (SEND, REPLY, 3),
    (WAIT, TOTAL, 0),
    (RUN, ADD, 0),
    (SEND, BOTH, 0),
    (WAIT, REPLY, 6),
    (RUN, OWN, 0),
    (WAIT, REPLY, 7),
    (WAIT, BOTH, 0),
    (WAIT, REPLY, 3),
    (RUN, FINISH, 0),
    (RUN, COMBINE, 0),
)


def local_paired(tokens, routes, centroid, ln_gain, ln_bias, w_in, b_in, w_out, b_out, cotangent):
    experts = lax.axis_size("expert")
    tok_count, width = tokens.shape
    capacity = 2 * tok_count // experts
    hidden = w_in.shape[2]
    core, chip = 1, 2
    order = Order()
    me = lax.axis_index("expert").astype(jnp.int32).reshape(1)
    made, moved = {}, {}
    sums = {MIDDLE: (), LEAVE: ()}
    final = [index for kind, what, index in plan if what == LEAVE and kind == RUN][-1]

    def dispatch(index):
        *parts, weights, params, tokens_near, cotangent_near, routes_near = order.kernel(
            functools.partial(dispatch_body, capacity, experts),
            [out(2 * capacity, width, bf16)] * experts
            + [
                out(width + hidden + 16, hidden, bf16),
                out(8, width, f32),
                out(tok_count, width, bf16),
                out(tok_count, width, bf16),
                out(1, tok_count, jnp.int32),
            ],
            (
                *(me, routes.reshape(1, tok_count), tokens, cotangent, w_in[0], w_out[0], b_in),
                *(centroid, ln_gain, ln_bias, b_out),
            ),
            "dispatch",
            scalars=1,
            far=10,
            scratch=[pltpu.SemaphoreType.DMA((10,))]
            + [pltpu.VMEM((1, x.shape[1]), bf16) for x in (b_in, centroid, ln_gain, ln_bias, b_out)],
        )
        order.fence = [params]
        for d, part in enumerate(parts):
            made[ROWS, d] = part
        moved[ROWS, 0] = parts[0]
        made[WEIGHTS, 0] = weights
        made[PARAMS] = params
        made[NEAR] = (me, routes_near, tokens_near, cotangent_near)

    def enter(index):
        ds = shares[index]
        made[SHARE, index] = order.kernel(
            functools.partial(enter_body, capacity, len(ds)),
            [out(2 * len(ds) * capacity, width, bf16)],
            (*[moved[ROWS, d] for d in ds], made[PARAMS]),
            "enter",
        )[0]

    def middle(index):
        own = [made[SHARE, i] for i in chunks[index]]
        half = sum(x.shape[0] for x in own) // 2
        got = order.kernel(
            functools.partial(middle_body, len(own), half, not sums[MIDDLE]),
            [out(2 * half, width, f32), out(2 * half, width, bf16)]
            + [out(2 * half, width, bf16)] * 2
            + [out(2 * half, hidden, bf16)] * 4
            + [out(8, hidden, f32)],
            (
                *own,
                *[moved[SHARE, i] for i in chunks[index]],
                *(made[WEIGHTS, 0], moved[WEIGHTS, 0]),
                *sums[MIDDLE],
            ),
            "middle",
            scratch=[pltpu.VMEM((2 * half, width), f32)] * 2,
            limit=24 << 20,
        )
        sums[MIDDLE] = (got[8],)
        made[MIDDLE, index] = got
        made[SUMS, index] = got[1]

    def leave(index):
        ds = [d for i in chunks[index] for d in shares[i]]
        *gone, total = order.kernel(
            functools.partial(leave_body, capacity, len(ds), not sums[LEAVE], index == final),
            [out(2 * capacity, width, bf16)] * len(ds) + [out(8, width, f32)],
            (
                *[moved[ROWS, d] for d in ds],
                *(made[MIDDLE, index][0], moved[SUMS, index], made[PARAMS]),
                *sums[LEAVE],
                *(sums[MIDDLE] if index == final else ()),
            ),
            "leave",
        )
        sums[LEAVE] = (total,)
        for d, x in zip(ds, gone):
            made[REPLY, d] = x
            if d == 0:
                moved[REPLY, d] = x
        made[TOTAL, 0] = total

    done = [index for kind, what, index in plan if what == MIDDLE and kind == RUN]

    def pick(*which):
        return [made[MIDDLE, c][i] for i in which for c in done]

    def sibling(index):
        (made[GRADS, 0],) = order.kernel(
            functools.partial(weights_body, len(pick(2))),
            [out(width + hidden, hidden, bf16)],
            pick(6, 7, 2, 3),
            "sibling_weights",
        )

    def own(index):
        made[OWN] = order.kernel(
            functools.partial(weights_body, len(pick(2))),
            [out(width, hidden, f32), out(hidden, width, f32), out(8, 128, f32)],
            (*pick(4, 5, 2, 3), moved[GRADS, 0]),
            "own_weights",
        )

    def add(index):
        total, came = made[TOTAL, 0], moved[TOTAL, 0]
        made[BIAS] = total[4:5] + came[5:6]
        made[BOTH, 0] = total + came

    def finish(index):
        made[FINISH] = made[BOTH, 0] + moved[BOTH, 0]

    def combine(index):
        made[COMBINE] = order.kernel(
            functools.partial(combine_body, capacity),
            [out(tok_count, width, bf16), out(tok_count, width, f32)],
            (*made[NEAR], *[moved[REPLY, d] for d in range(experts)]),
            "combine",
            scalars=1,
        )

    kernels = {
        DISPATCH: dispatch,
        ENTER: enter,
        MIDDLE: middle,
        LEAVE: leave,
        SIBLING: sibling,
        OWN: own,
        ADD: add,
        FINISH: finish,
        COMBINE: combine,
    }
    for kind, what, index in plan:
        if kind == RUN:
            kernels[what](index)
        elif kind == WAIT:
            order.wait(moved[what, index])
        elif what in (ROWS, REPLY):
            moved[what, index] = order.start(made[what, index], "expert", index, what)
        else:
            offset = core if what in (WEIGHTS, GRADS, TOTAL) else chip
            moved[what, index] = order.start(made[what, index], "batch", offset, what, index)
    mixed, tokens_grad = made[COMBINE]
    total = made[FINISH]
    return (
        mixed,
        tokens_grad,
        total[0:1],
        total[1:2],
        total[2:3],
        made[OWN][0][None],
        made[BIAS],
        made[OWN][1][None],
        total[3:4],
    )


def local(tokens, routes, centroid, ln_gain, ln_bias, w_in, b_in, w_out, b_out, cotangent):
    experts = lax.axis_size("expert")
    tok_count, width = tokens.shape
    capacity = 2 * tok_count // experts
    power_of_two = experts & (experts - 1) == 0
    paired = (
        lax.axis_size("batch") == 4
        and experts == sum(len(ds) for ds in shares)
        and power_of_two
        and capacity % 16 == 0
        and capacity <= 128
        and width == w_in.shape[2]
        and width % 128 == 0
    )
    plan = local_paired if paired else local_general
    return plan(
        tokens, routes, centroid, ln_gain, ln_bias, w_in, b_in, w_out, b_out, cotangent
    )


def solution(mesh):
    in_specs = (
        P(("expert", "batch"), None),
        P(("expert", "batch"), None),
        P("expert", None),
        P("expert", None),
        P("expert", None),
        P("expert", None, "batch"),
        P("expert", "batch"),
        P("expert", "batch", None),
        P("expert", None),
        P(("expert", "batch"), None),
    )
    out_specs = (
        P(("expert", "batch"), None),
        P(("expert", "batch"), None),
        P("expert", None),
        P("expert", None),
        P("expert", None),
        P("expert", None, "batch"),
        P("expert", "batch"),
        P("expert", "batch", None),
        P("expert", None),
    )
    return jax.shard_map(local, mesh=mesh, in_specs=in_specs, out_specs=out_specs, check_vma=False)
```

```python
import functools

import jax
import jax.numpy as jnp
from jax import lax
from jax.experimental import pallas as pl
from jax.experimental.pallas import tpu as pltpu
from jax.sharding import PartitionSpec as P

epsilon = 1e-05
root_half = 0.7071067811865476
gauss_norm = 0.3989422804014327


def gelu_parts(pre_act):
    gelu_value = jax.nn.gelu(pre_act, approximate=False)
    gelu_slope = (
        0.5 * (1.0 + lax.erf(pre_act * root_half))
        + pre_act * jnp.exp(-0.5 * pre_act * pre_act) * gauss_norm
    )
    return (gelu_value.astype(jnp.bfloat16), gelu_slope)


def contract_first(left, right):
    return lax.dot_general(
        left, right, (((0,), (0,)), ((), ())), preferred_element_type=jnp.float32
    )


def contract_last(left, right):
    return lax.dot_general(
        left, right, (((1,), (1,)), ((), ())), preferred_element_type=jnp.float32
    )


def local_general(tokens, routes, centroid, ln_gain, ln_bias, w_in, b_in, w_out, b_out, cotangent):
    experts = lax.axis_size("expert")
    tok_count = tokens.shape[0]
    model_width = tokens.shape[1]
    capacity = max(2, 2 * tok_count // experts)
    row_count = experts * capacity
    route_ids = routes[:, 0]
    onehot = (route_ids[:, None] == jnp.arange(experts, dtype=jnp.int32)[None, :]).astype(jnp.int32)
    before = jnp.cumsum(onehot, axis=0) - onehot
    rank_in = jnp.sum(before * onehot, axis=1)
    target = route_ids * capacity + rank_in
    placing = (jnp.arange(row_count, dtype=jnp.int32)[:, None] == target[None, :]).astype(
        jnp.bfloat16
    )
    outgoing = jnp.dot(placing, tokens, preferred_element_type=jnp.float32).astype(jnp.bfloat16)
    arrived = lax.all_to_all(
        outgoing.reshape(experts, capacity, model_width),
        "expert",
        split_axis=0,
        concat_axis=0,
        tiled=True,
    )
    arrived = arrived.reshape(row_count, model_width)
    hidden_in = arrived.astype(jnp.float32)
    center = jnp.mean(hidden_in, axis=1, keepdims=True)
    spread = jnp.mean((hidden_in - center) * (hidden_in - center), axis=1, keepdims=True)
    inv_std = lax.rsqrt(spread + epsilon)
    normed = (hidden_in - center) * inv_std
    gain_row = ln_gain[0].astype(jnp.float32)
    shift_row = ln_bias[0].astype(jnp.float32)
    cent_row = centroid[0].astype(jnp.float32)
    b_last = b_out[0].astype(jnp.float32)
    lowered = (normed * gain_row + shift_row).astype(jnp.bfloat16)
    gate_logit = jnp.dot(arrived, centroid[0], preferred_element_type=jnp.float32)
    mixing = jax.nn.sigmoid(gate_logit)
    w_first = w_in[0]
    w_second = w_out[0]
    b_first = b_in[0].astype(jnp.float32)
    inputs_all = lax.all_gather(lowered, "batch", axis=0, tiled=True)
    row_piece = inputs_all
    piece_act, unused = gelu_parts(
        jnp.dot(row_piece, w_first, preferred_element_type=jnp.float32) + b_first
    )
    branch = (
        lax.psum_scatter(
            jnp.dot(piece_act, w_second, preferred_element_type=jnp.float32).astype(jnp.bfloat16),
            "batch",
            scatter_dimension=0,
            tiled=True,
        ).astype(jnp.float32)
        + b_last
    )
    expert_out = hidden_in + branch
    reply_rows = (mixing[:, None] * expert_out).astype(jnp.bfloat16)
    returned = lax.all_to_all(
        reply_rows.reshape(experts, capacity, model_width),
        "expert",
        split_axis=0,
        concat_axis=0,
        tiled=True,
    )
    returned = returned.reshape(row_count, model_width)
    mixed = (tokens.astype(jnp.float32) + contract_first(placing, returned)).astype(jnp.bfloat16)
    grad_out = jnp.dot(placing, cotangent, preferred_element_type=jnp.float32).astype(jnp.bfloat16)
    grad_rows = lax.all_to_all(
        grad_out.reshape(experts, capacity, model_width),
        "expert",
        split_axis=0,
        concat_axis=0,
        tiled=True,
    )
    grad_rows = grad_rows.reshape(row_count, model_width).astype(jnp.float32)
    gate_grad = jnp.sum(grad_rows * expert_out, axis=1) * mixing * (1.0 - mixing)
    direct = grad_rows * mixing[:, None]
    branch_grad = direct.astype(jnp.bfloat16)
    b_out_part = jnp.sum(branch_grad.astype(jnp.float32), axis=0)
    centroid_part = jnp.sum(gate_grad[:, None] * hidden_in, axis=0)
    grads_all = lax.all_gather(branch_grad, "batch", axis=0, tiled=True)
    activated, gelu_slope = gelu_parts(
        jnp.dot(inputs_all, w_first, preferred_element_type=jnp.float32) + b_first
    )
    pre_grad = (contract_last(grads_all, w_second) * gelu_slope).astype(jnp.bfloat16)
    w_out_grad = contract_first(activated, grads_all)
    w_in_grad = contract_first(inputs_all, pre_grad)
    b_in_grad = jnp.sum(pre_grad.astype(jnp.float32), axis=0)
    row_piece = pre_grad
    normed_grad = lax.psum_scatter(
        contract_last(row_piece, w_first), "batch", scatter_dimension=0, tiled=True
    )
    gain_part = jnp.sum(normed_grad * normed, axis=0)
    bias_part = jnp.sum(normed_grad, axis=0)
    scaled = normed_grad * gain_row
    ln_grad = inv_std * (
        scaled
        - jnp.mean(scaled, axis=1, keepdims=True)
        - normed * jnp.mean(scaled * normed, axis=1, keepdims=True)
    )
    input_grad = direct + gate_grad[:, None] * cent_row + ln_grad
    outgoing_grads = input_grad.astype(jnp.bfloat16).reshape(experts, capacity, model_width)
    arrived_grads = lax.all_to_all(
        outgoing_grads, "expert", split_axis=0, concat_axis=0, tiled=True
    ).reshape(row_count, model_width)
    tokens_grad = cotangent.astype(jnp.float32) + contract_first(placing, arrived_grads)
    small_sums = lax.psum((centroid_part, gain_part, bias_part, b_out_part), "batch")
    return (
        mixed,
        tokens_grad,
        small_sums[0][None],
        small_sums[1][None],
        small_sums[2][None],
        w_in_grad[None],
        b_in_grad[None],
        w_out_grad[None],
        small_sums[3][None],
    )


f32 = jnp.float32
bf16 = jnp.bfloat16

erfc_step = 0.3 * root_half
erfc_half = tuple(
    0.5 * c
    for c in (
        0.16918935705144628,
        0.1706908732382945,
        0.14852168107322075,
        0.21417961390291307,
        -0.09282143256694776,
        0.5449597059025907,
        -0.5097655323576785,
        0.48429815524087755,
        -0.12925243016104992,
    )
)


def gelu_and_slope(a):
    bell = jnp.exp(-0.5 * a * a)
    t = 1.0 / (1.0 + erfc_step * jnp.abs(a))
    poly = erfc_half[-1]
    for c in erfc_half[-2::-1]:
        poly = poly * t + c
    tail = poly * t * bell
    below = jnp.where(a < 0.0, tail, 1.0 - tail)
    return a * below, below + a * bell * gauss_norm


def whole():
    return pl.BlockSpec(memory_space=pltpu.VMEM)


def call(body, outs, args, name, scratch=(), scalars=0, far=0, limit=12 << 20, after=(), flops=0):
    count, extra = len(args), len(after)
    args = tuple(
        pltpu.with_memory_space_constraint(x, pltpu.HBM) if scalars <= i < scalars + far else x
        for i, x in enumerate(args)
    )

    def run(*refs):
        body(*refs[:count], *refs[count + extra :])

    return pl.pallas_call(
        run,
        out_shape=tuple(outs),
        in_specs=[pl.BlockSpec(memory_space=pltpu.SMEM)] * scalars
        + [pl.BlockSpec(memory_space=pltpu.HBM)] * far
        + [whole()] * (count - scalars - far)
        + [pl.BlockSpec(memory_space=pl.ANY)] * extra,
        out_specs=tuple(whole() for _ in outs),
        scratch_shapes=list(scratch),
        compiler_params=pltpu.CompilerParams(vmem_limit_bytes=limit),
        cost_estimate=pl.CostEstimate(flops=flops, bytes_accessed=0, transcendentals=0),
        name=name,
    )(*args, *after)


def out(rows, cols, dtype):
    return jax.ShapeDtypeStruct((rows, cols), dtype)


def iota(shape, dim):
    return lax.broadcasted_iota(jnp.int32, shape, dim)


def slot_row(capacity, me, row):
    n = row.shape[1]
    wide = jnp.broadcast_to(row, (n, n))
    i, j = iota((n, n), 0), iota((n, n), 1)
    col = jnp.sum(jnp.where(i == j, wide, 0), axis=1, keepdims=True)
    rank = jnp.sum(((col == wide) & (i < j)).astype(jnp.int32), axis=0, keepdims=True)
    return jnp.bitwise_xor(row, me) * capacity + rank


def slot_col(capacity, me, row):
    n = row.shape[1]
    wide = jnp.broadcast_to(row, (n, n))
    i, j = iota((n, n), 0), iota((n, n), 1)
    col = jnp.sum(jnp.where(i == j, wide, 0), axis=1, keepdims=True)
    rank = jnp.sum(((col == wide) & (j < i)).astype(jnp.int32), axis=1, keepdims=True)
    return jnp.bitwise_xor(col, me) * capacity + rank


def dispatch_body(capacity, experts, me, *refs):
    far, parts, rest = refs[:10], refs[10 : 10 + experts], refs[10 + experts :]
    weights, params, tokens, cotangent, routes, sems, *lines = rest
    rows_in, rows_out = far[3].shape[0], far[4].shape[0]
    places = [
        routes,
        tokens,
        cotangent,
        weights.at[0:rows_in],
        weights.at[rows_in : rows_in + rows_out],
        *lines,
    ]
    copies = [
        pltpu.make_async_copy(x, place, sems.at[i])
        for i, (x, place) in enumerate(zip(far, places))
    ]
    for copy in copies:
        copy.start()
    slots = experts * capacity
    copies[0].wait()
    n = routes.shape[1]
    slot = slot_row(capacity, me[0], routes[...])
    place = (iota((slots, n), 0) == jnp.broadcast_to(slot, (slots, n))).astype(bf16)
    copies[1].wait()
    rows = jnp.dot(place, tokens[...], preferred_element_type=f32).astype(bf16)
    for d, part in enumerate(parts):
        part[0:capacity, :] = rows[d * capacity : (d + 1) * capacity, :]
    copies[2].wait()
    grads = jnp.dot(place, cotangent[...], preferred_element_type=f32).astype(bf16)
    for d, part in enumerate(parts):
        part[capacity:, :] = grads[d * capacity : (d + 1) * capacity, :]
    for copy in copies[3:]:
        copy.wait()
    spare = weights.shape[0] - rows_in - rows_out
    weights[rows_in + rows_out :, :] = jnp.broadcast_to(lines[0][...], (spare, lines[0].shape[1]))
    for i, line in enumerate(lines[1:]):
        params[i : i + 1, :] = line[...].astype(f32)
    params[len(lines) - 1 :, :] = jnp.zeros_like(params[len(lines) - 1 :, :])


def row_mean(x):
    return jnp.mean(x, axis=1, keepdims=True)


def norm_parts(h):
    center = row_mean(h)
    spread = row_mean((h - center) * (h - center))
    inv_std = lax.rsqrt(spread + epsilon)
    return (h - center) * inv_std, inv_std


def gate(h, cent):
    return jax.nn.sigmoid(jnp.sum(h * cent, axis=1, keepdims=True))


def enter_body(capacity, count, *refs):
    parts, (params, both) = refs[:count], refs[count:]
    cent, gain, shift = (params[i : i + 1, :] for i in range(3))
    half = count * capacity
    for j, part in enumerate(parts):
        h = part[0:capacity, :].astype(f32)
        normed, unused = norm_parts(h)
        lowered = normed * gain + shift
        at = j * capacity
        both[at : at + capacity, :] = lowered.astype(bf16)
        mixing = gate(h, cent)
        both[half + at : half + at + capacity, :] = (
            part[capacity:, :].astype(f32) * mixing
        ).astype(bf16)


def middle_body(count, half, first, *refs):
    own, other, refs = refs[:count], refs[count : 2 * count], refs[2 * count :]
    quarters, refs = refs[:2], refs[2:]
    if not first:
        before, refs = refs[0], refs[1:]
    keep, send, n_all, dz_all, u0, da0, u1, da1, sums, z_acc, dn_acc = refs
    at = 0
    for both in own + other:
        rows = both.shape[0] // 2
        n_all[at : at + rows, :] = both[0:rows, :]
        dz_all[at : at + rows, :] = both[rows:, :]
        at += rows
    width, hidden = n_all.shape[1], u0.shape[1]
    for q, (weights, u_ref, da_ref) in enumerate(
        ((quarters[0], u0, da0), (quarters[1], u1, da1))
    ):
        wi, wo = weights.at[0:width], weights.at[width : width + hidden]
        b = weights.at[width + hidden : width + hidden + 1]
        a = jnp.dot(n_all[...], wi[...], preferred_element_type=f32) + b[...].astype(f32)
        t = contract_last(dz_all[...], wo[...])
        u, slope = gelu_and_slope(a)
        u = u.astype(bf16)
        u_ref[...] = u
        z = jnp.dot(u, wo[...], preferred_element_type=f32)
        da = (t * slope).astype(bf16)
        da_ref[...] = da
        dn = contract_last(da, wi[...])
        total = jnp.sum(da.astype(f32), axis=0, keepdims=True)
        if not first:
            total = total + before[q : q + 1, :]
        sums[q : q + 1, :] = total
        if q == 0:
            z_acc[...] = z
            dn_acc[...] = dn
        else:
            z_acc[...] += z
            dn_acc[...] += dn
    sums[2:, :] = jnp.zeros_like(sums[2:, :])
    keep[0:half, :] = z_acc[0:half, :]
    keep[half:, :] = dn_acc[0:half, :]
    send[0:half, :] = z_acc[half:, :].astype(bf16)
    send[half:, :] = dn_acc[half:, :].astype(bf16)


def leave_body(capacity, count, first, last, *refs):
    parts, refs = refs[:count], refs[count:]
    (keep, came, params), refs = refs[:3], refs[3:]
    if not first:
        before, refs = refs[0], refs[1:]
    if last:
        hidden_sums, refs = refs[0], refs[1:]
    replies, sums = refs[:count], refs[count]
    half = count * capacity
    cent_row, gain_row, last_row = (params[i : i + 1, :] for i in (0, 1, 3))
    totals = [0.0, 0.0, 0.0, 0.0]
    for j, part in enumerate(parts):
        at = j * capacity
        h = part[0:capacity, :].astype(f32)
        g = part[capacity:, :].astype(f32)
        z = keep[at : at + capacity, :] + came[at : at + capacity, :].astype(f32)
        dn = (
            keep[half + at : half + at + capacity, :]
            + came[half + at : half + at + capacity, :].astype(f32)
        )
        f = h + (z + last_row)
        mixing = gate(h, cent_row)
        replies[j][0:capacity, :] = (mixing * f).astype(bf16)
        p = jnp.sum(g * f, axis=1, keepdims=True) * mixing * (1.0 - mixing)
        direct = g * mixing
        normed, inv_std = norm_parts(h)
        w = dn * gain_row
        dh = (
            direct
            + p * cent_row
            + inv_std * (w - row_mean(w) - normed * row_mean(w * normed))
        )
        replies[j][capacity:, :] = dh.astype(bf16)
        for i, rows in enumerate((p * h, dn * normed, dn, direct.astype(bf16).astype(f32))):
            totals[i] = totals[i] + jnp.sum(rows, axis=0, keepdims=True)
    for i, total in enumerate(totals):
        if not first:
            total = total + before[i : i + 1, :]
        sums[i : i + 1, :] = total
    if last:
        sums[4:6, :] = hidden_sums[0:2, :]
        sums[6:, :] = jnp.zeros_like(sums[6:, :])
    else:
        sums[4:, :] = jnp.zeros_like(sums[4:, :])


def weights_body(chunks, *refs):
    u, da, n, dz = (refs[i * chunks : (i + 1) * chunks] for i in range(4))
    rest = refs[4 * chunks :]
    width, hidden = n[0].shape[1], u[0].shape[1]
    step = 512
    for k, (left, right) in enumerate(((n, da), (u, dz))):
        size = left[0].shape[1]
        grad, offset = (rest[0], k * width) if len(rest) == 1 else (rest[1 + k], 0)

        def some(i, unused, left=left, right=right, grad=grad, offset=offset, k=k):
            at = pl.multiple_of(i * step, step)
            total = contract_first(
                jnp.concatenate([x[:, pl.ds(at, step)] for x in left], axis=0),
                jnp.concatenate([x[...] for x in right], axis=0),
            )
            if len(rest) == 4:
                total = total + rest[0][pl.ds(k * width + at, step), :].astype(f32)
            grad[pl.ds(offset + at, step), :] = total.astype(grad.dtype)
            return unused

        lax.fori_loop(0, size // step, some, 0)
    if len(rest) == 4:
        rest[3][...] = jnp.zeros_like(rest[3])


def combine_body(capacity, me, routes, tokens, cotangent, *refs):
    replies, (mixed, tokens_grad) = refs[:-2], refs[-2:]
    slots = len(replies) * capacity
    n = routes.shape[1]
    slot = slot_col(capacity, me[0], routes[...])
    place = (iota((n, slots), 1) == jnp.broadcast_to(slot, (n, slots))).astype(bf16)
    rows = jnp.concatenate([x[0:capacity, :] for x in replies], axis=0)
    grads = jnp.concatenate([x[capacity:, :] for x in replies], axis=0)
    mixed[...] = (
        tokens[...].astype(f32) + jnp.dot(place, rows, preferred_element_type=f32)
    ).astype(bf16)
    tokens_grad[...] = cotangent[...].astype(f32) + jnp.dot(
        place, grads, preferred_element_type=f32
    )


class Order:
    def __init__(self):
        self.fence = []
        self.flops = 0

    def kernel(self, body, outs, args, name, **more):
        mine = {id(x) for x in args}
        after = [x for x in self.fence if id(x) not in mine]
        got = call(body, outs, args, name, after=after, flops=self.flops, **more)
        self.fence = [got[-1]]
        return got

    def start(self, x, axis, offset, what, index=None):
        others = [y for y in self.fence if y is not x]
        if others:
            x = lax.optimization_barrier((x, *others))[0]
        size = lax.axis_size(axis)
        with jax.named_scope(f"t{what}_{offset if index is None else index}"):
            return lax.ppermute(x, axis, [(i, i ^ offset) for i in range(size)])

    def wait(self, array):
        self.fence = self.fence + [array]


(
    DISPATCH,
    ENTER,
    MIDDLE,
    LEAVE,
    SIBLING,
    OWN,
    ADD,
    FINISH,
    COMBINE,
    ROWS,
    SHARE,
    SUMS,
    REPLY,
    WEIGHTS,
    GRADS,
    TOTAL,
    BOTH,
    PARAMS,
    NEAR,
    BIAS,
) = range(20)
RUN, SEND, WAIT = range(3)

shares = ((0,), (6,), (1, 5), (3, 4), (2, 7))
chunks = ((0, 1), (2,), (3,), (4,))

work = {(LEAVE, 3): 40}

plan = (
    (RUN, DISPATCH, 0),
    (SEND, ROWS, 4),
    (SEND, WEIGHTS, 0),
    (SEND, ROWS, 3),
    (WAIT, WEIGHTS, 0),
    (SEND, ROWS, 5),
    (RUN, ENTER, 0),
    (SEND, SHARE, 0),
    (SEND, ROWS, 1),
    (SEND, ROWS, 6),
    (SEND, ROWS, 2),
    (WAIT, ROWS, 4),
    (WAIT, ROWS, 3),
    (RUN, ENTER, 3),
    (SEND, SHARE, 3),
    (SEND, ROWS, 7),
    (WAIT, SHARE, 0),
    (WAIT, ROWS, 1),
    (WAIT, ROWS, 5),
    (RUN, ENTER, 2),
    (SEND, SHARE, 2),
    (WAIT, SHARE, 3),
    (RUN, MIDDLE, 2),
    (SEND, SUMS, 2),
    (WAIT, SHARE, 2),
    (RUN, MIDDLE, 1),
    (SEND, SUMS, 1),
    (WAIT, ROWS, 6),
    (RUN, ENTER, 1),
    (WAIT, ROWS, 2),
    (SEND, SHARE, 1),
    (WAIT, ROWS, 7),
    (RUN, ENTER, 4),
    (SEND, SHARE, 4),
    (WAIT, SUMS, 2),
    (RUN, LEAVE, 2),
    (SEND, REPLY, 3),
    (SEND, REPLY, 4),
    (WAIT, SUMS, 1),
    (RUN, LEAVE, 1),
    (WAIT, SHARE, 1),
    (SEND, REPLY, 5),
    (RUN, MIDDLE, 0),
    (SEND, REPLY, 1),
    (WAIT, REPLY, 4),
    (SEND, SUMS, 0),
    (WAIT, SHARE, 4),
    (RUN, MIDDLE, 3),
    (SEND, SUMS, 3),
    (RUN, SIBLING, 0),
    (WAIT, SUMS, 0),
    (WAIT, REPLY, 3),
    (WAIT, REPLY, 5),
    (SEND, GRADS, 0),
    (RUN, LEAVE, 0),
    (SEND, REPLY, 6),
    (WAIT, REPLY, 1),
    (WAIT, SUMS, 3),
    (RUN, LEAVE, 3),
    (SEND, REPLY, 2),
    (SEND, TOTAL, 0),
    (WAIT, GRADS, 0),
    (WAIT, TOTAL, 0),
    (RUN, ADD, 0),
    (SEND, REPLY, 7),
    (SEND, BOTH, 0),
    (WAIT, REPLY, 6),
    (RUN, OWN, 0),
    (WAIT, REPLY, 7),
    (WAIT, BOTH, 0),
    (WAIT, REPLY, 2),
    (RUN, FINISH, 0),
    (RUN, COMBINE, 0),
)


def local_paired(tokens, routes, centroid, ln_gain, ln_bias, w_in, b_in, w_out, b_out, cotangent):
    experts = lax.axis_size("expert")
    tok_count, width = tokens.shape
    capacity = 2 * tok_count // experts
    hidden = w_in.shape[2]
    core, chip = 1, 2
    order = Order()
    me = lax.axis_index("expert").astype(jnp.int32).reshape(1)
    made, moved = {}, {}
    sums = {MIDDLE: (), LEAVE: ()}
    final = [index for kind, what, index in plan if what == LEAVE and kind == RUN][-1]

    def dispatch(index):
        *parts, weights, params, tokens_near, cotangent_near, routes_near = order.kernel(
            functools.partial(dispatch_body, capacity, experts),
            [out(2 * capacity, width, bf16)] * experts
            + [
                out(width + hidden + 16, hidden, bf16),
                out(8, width, f32),
                out(tok_count, width, bf16),
                out(tok_count, width, bf16),
                out(1, tok_count, jnp.int32),
            ],
            (
                *(me, routes.reshape(1, tok_count), tokens, cotangent, w_in[0], w_out[0], b_in),
                *(centroid, ln_gain, ln_bias, b_out),
            ),
            "dispatch",
            scalars=1,
            far=10,
            scratch=[pltpu.SemaphoreType.DMA((10,))]
            + [pltpu.VMEM((1, x.shape[1]), bf16) for x in (b_in, centroid, ln_gain, ln_bias, b_out)],
        )
        order.fence = [params]
        for d, part in enumerate(parts):
            made[ROWS, d] = part
        moved[ROWS, 0] = parts[0]
        made[WEIGHTS, 0] = weights
        made[PARAMS] = params
        made[NEAR] = (me, routes_near, tokens_near, cotangent_near)

    def enter(index):
        ds = shares[index]
        made[SHARE, index] = order.kernel(
            functools.partial(enter_body, capacity, len(ds)),
            [out(2 * len(ds) * capacity, width, bf16)],
            (*[moved[ROWS, d] for d in ds], made[PARAMS]),
            "enter",
        )[0]

    def middle(index):
        own = [made[SHARE, i] for i in chunks[index]]
        half = sum(x.shape[0] for x in own) // 2
        got = order.kernel(
            functools.partial(middle_body, len(own), half, not sums[MIDDLE]),
            [out(2 * half, width, f32), out(2 * half, width, bf16)]
            + [out(2 * half, width, bf16)] * 2
            + [out(2 * half, hidden, bf16)] * 4
            + [out(8, hidden, f32)],
            (
                *own,
                *[moved[SHARE, i] for i in chunks[index]],
                *(made[WEIGHTS, 0], moved[WEIGHTS, 0]),
                *sums[MIDDLE],
            ),
            "middle",
            scratch=[pltpu.VMEM((2 * half, width), f32)] * 2,
            limit=24 << 20,
        )
        sums[MIDDLE] = (got[8],)
        made[MIDDLE, index] = got
        made[SUMS, index] = got[1]

    def leave(index):
        ds = [d for i in chunks[index] for d in shares[i]]
        *gone, total = order.kernel(
            functools.partial(leave_body, capacity, len(ds), not sums[LEAVE], index == final),
            [out(2 * capacity, width, bf16)] * len(ds) + [out(8, width, f32)],
            (
                *[moved[ROWS, d] for d in ds],
                *(made[MIDDLE, index][0], moved[SUMS, index], made[PARAMS]),
                *sums[LEAVE],
                *(sums[MIDDLE] if index == final else ()),
            ),
            "leave",
        )
        sums[LEAVE] = (total,)
        for d, x in zip(ds, gone):
            made[REPLY, d] = x
            if d == 0:
                moved[REPLY, d] = x
        made[TOTAL, 0] = total

    done = [index for kind, what, index in plan if what == MIDDLE and kind == RUN]

    def pick(*which):
        return [made[MIDDLE, c][i] for i in which for c in done]

    def sibling(index):
        (made[GRADS, 0],) = order.kernel(
            functools.partial(weights_body, len(pick(2))),
            [out(width + hidden, hidden, bf16)],
            pick(6, 7, 2, 3),
            "sibling_weights",
        )

    def own(index):
        made[OWN] = order.kernel(
            functools.partial(weights_body, len(pick(2))),
            [out(width, hidden, f32), out(hidden, width, f32), out(8, 128, f32)],
            (*pick(4, 5, 2, 3), moved[GRADS, 0]),
            "own_weights",
        )

    def add(index):
        total, came = made[TOTAL, 0], moved[TOTAL, 0]
        made[BIAS] = total[4:5] + came[5:6]
        made[BOTH, 0] = total + came

    def finish(index):
        made[FINISH] = made[BOTH, 0] + moved[BOTH, 0]

    def combine(index):
        made[COMBINE] = order.kernel(
            functools.partial(combine_body, capacity),
            [out(tok_count, width, bf16), out(tok_count, width, f32)],
            (*made[NEAR], *[moved[REPLY, d] for d in range(experts)]),
            "combine",
            scalars=1,
        )

    kernels = {
        DISPATCH: dispatch,
        ENTER: enter,
        MIDDLE: middle,
        LEAVE: leave,
        SIBLING: sibling,
        OWN: own,
        ADD: add,
        FINISH: finish,
        COMBINE: combine,
    }
    for kind, what, index in plan:
        if kind == RUN:
            order.flops = 10**9 * work.get((what, index), 0)
            kernels[what](index)
        elif kind == WAIT:
            order.wait(moved[what, index])
        elif what in (ROWS, REPLY):
            moved[what, index] = order.start(made[what, index], "expert", index, what)
        else:
            offset = core if what in (WEIGHTS, GRADS, TOTAL) else chip
            moved[what, index] = order.start(made[what, index], "batch", offset, what, index)
    mixed, tokens_grad = made[COMBINE]
    total = made[FINISH]
    return (
        mixed,
        tokens_grad,
        total[0:1],
        total[1:2],
        total[2:3],
        made[OWN][0][None],
        made[BIAS],
        made[OWN][1][None],
        total[3:4],
    )


def local(tokens, routes, centroid, ln_gain, ln_bias, w_in, b_in, w_out, b_out, cotangent):
    experts = lax.axis_size("expert")
    tok_count, width = tokens.shape
    capacity = 2 * tok_count // experts
    power_of_two = experts & (experts - 1) == 0
    paired = (
        lax.axis_size("batch") == 4
        and experts == sum(len(ds) for ds in shares)
        and power_of_two
        and capacity % 16 == 0
        and capacity <= 128
        and width == w_in.shape[2]
        and width % 128 == 0
    )
    plan = local_paired if paired else local_general
    return plan(
        tokens, routes, centroid, ln_gain, ln_bias, w_in, b_in, w_out, b_out, cotangent
    )


def solution(mesh):
    in_specs = (
        P(("expert", "batch"), None),
        P(("expert", "batch"), None),
        P("expert", None),
        P("expert", None),
        P("expert", None),
        P("expert", None, "batch"),
        P("expert", "batch"),
        P("expert", "batch", None),
        P("expert", None),
        P(("expert", "batch"), None),
    )
    out_specs = (
        P(("expert", "batch"), None),
        P(("expert", "batch"), None),
        P("expert", None),
        P("expert", None),
        P("expert", None),
        P("expert", None, "batch"),
        P("expert", "batch"),
        P("expert", "batch", None),
        P("expert", None),
    )
    return jax.shard_map(local, mesh=mesh, in_specs=in_specs, out_specs=out_specs, check_vma=False)
```
